256 devices in a mesh: seq: 128 (over z, y, x_lo, core), head: 2 (over x_hi).
Axes of the slice: x: 4 (x_hi: 2, x_lo: 2; x = x_hi * 2 + x_lo), y: 4, z: 8, core: 2. Of those that a mesh axis runs over, the one named last changes fastest.
Arguments:
- latents: bfloat16 [32768, 1024], P('seq', 'head'), may hold values from -6 to 6
- known: bfloat16 [32768, 1024], P('seq', 'head'), may hold values from -6 to 6
- seam_mask: int32 [32768], P('seq'), may hold values 0 or 1
- timesteps: int32 [3], replicated, may hold values from 302 to 800, as said below
- block_lists: int32 [256, 6], P('seq'), may hold values from -1 to 255, as said below
- guidance: bfloat16 [2, 1024, 1024], P(None, 'seq'), may hold values from -7 to 7
- modulation_weight: bfloat16 [256, 4, 1024], replicated, may hold values from -0.75 to 0.75
- self_weight: bfloat16 [1024, 3, 1024], P(None, None, 'head')
- self_out_weight: bfloat16 [1024, 1024], P('head'), may hold values from -0.1875 to 0.1875
- cross_weight: bfloat16 [1024, 3, 1024], P(None, None, 'head')
- cross_out_weight: bfloat16 [1024, 1024], P('head'), may hold values from -0.1875 to 0.1875
Outputs:
- denoised: bfloat16 [32768, 1024], P('seq', 'head')
The draws below stay inside these ranges and needn't reach their ends.
Inputs may be any that keep to these rules, and one draw needn't show every extreme that they name: `block_lists`: row b starts with b itself, followed by distinct blocks of the query's own tile or of the tiles 1 and 4 away on either side along the closed band of 128 tiles; the rest of the row is -1. Some rows hold 6 blocks. `timesteps`: strictly falling.
All inputs are finite; a program needn't handle non-finite values. No bound on the sum of `seam_mask` on one device may be relied on, other than what follows from the above.
Results may differ from the reference program's by a relative error of at most 0.011.
Values may be sent and summed in bfloat16 or wider, within the bound.
A program may use at most 128 MiB of HBM per device.

```python
import math
import jax
import jax.numpy as jnp
from jax import lax

D = 1024
HEADS = 16
HEAD_DIM = 64
FREQ = 256
BLOCK = 128
MAXK = 6
ROW = 4
STEPS = 2
TOK_DEV = 256
TOKENS = 32768
NBLK = 256
G = 1024


def latent_base(key):
    fresh = jax.random.normal(jax.random.fold_in(key, 11), (TOKENS, D), jnp.float32)
    return jnp.clip(fresh, -6.0, 6.0)


def draw_latents(key, part):
    return latent_base(key).astype(jnp.bfloat16)


def draw_guidance(key, part):
    fresh = jnp.clip(jax.random.normal(jax.random.fold_in(key, 12), (STEPS, G, D), jnp.float32), -6.0, 6.0)
    stride = TOKENS // G
    copied = jnp.roll(latent_base(key)[::stride], G // 2, axis=0)
    result = copied[None, :, :] + 0.5 * fresh
    return jnp.clip(result, -7.0, 7.0).astype(jnp.bfloat16)


def projection(key, salt, aligned):
    base = jax.random.normal(jax.random.fold_in(key, salt), (D, 3, D), jnp.float32) / math.sqrt(D)
    query_part = 2.0 * base[:, 0]
    if aligned:
        key_part = query_part + 0.3 * base[:, 1]
    else:
        key_part = base[:, 1]
    return jnp.stack([query_part, key_part, base[:, 2]], axis=1).astype(jnp.bfloat16)


def draw_self_weight(key, part):
    return projection(key, 31, False)


def draw_cross_weight(key, part):
    return projection(key, 41, True)


def draw_timesteps(key, part):
    start = jnp.full((1,), 800, jnp.int32)
    gaps = jax.random.randint(jax.random.fold_in(key, 52), (STEPS,), 50, 250)
    return jnp.concatenate([start, start - jnp.cumsum(gaps)]).astype(jnp.int32)


def draw_block_lists(key, part):
    per_tile = TOK_DEV // BLOCK
    tiles = NBLK // per_tile
    block = jnp.arange(NBLK, dtype=jnp.int32)
    tile = block // per_tile
    moves = jnp.array([0, -1, 1, -ROW, ROW], dtype=jnp.int32)
    target = (tile[:, None] + moves[None, :]) % tiles
    within = jnp.arange(per_tile, dtype=jnp.int32)
    candidate = (target[:, :, None] * per_tile + within[None, None, :]).reshape(NBLK, 5 * per_tile)
    is_own = candidate == block[:, None]
    ranking = jax.random.randint(jax.random.fold_in(key, 61), (NBLK, 5 * per_tile), 0, 1 << 20) * 128
    ranking = ranking + jnp.arange(5 * per_tile, dtype=jnp.int32)[None, :]
    ranking = jnp.where(is_own, 1 << 28, ranking)
    order = jnp.argsort(ranking, axis=1)
    others = jnp.take_along_axis(candidate, order, axis=1)[:, :MAXK - 1]
    heat = jax.random.randint(jax.random.fold_in(key, 62), (tiles,), 0, 4)
    chosen_tile = jax.random.randint(jax.random.fold_in(key, 63), (), 0, tiles)
    hot_tile = (heat == 0) | (jnp.arange(tiles, dtype=jnp.int32) == chosen_tile)
    count = 1 + jax.random.randint(jax.random.fold_in(key, 64), (NBLK,), 0, MAXK - 1)
    count = jnp.where(hot_tile[tile], MAXK, count)
    listed = jnp.concatenate([block[:, None], others], axis=1)
    column = jnp.arange(MAXK, dtype=jnp.int32)[None, :]
    return jnp.where(column < count[:, None], listed, -1).astype(jnp.int32)


def touch_ends(values, stream_key, least, high):
    dims = values.shape
    index_at = [jax.random.randint(jax.random.fold_in(stream_key, axis), (), 0, dims[axis]) for axis in range(len(dims))]
    values = values.at[tuple(index_at)].set(least)
    longest = dims.index(max(dims))
    index_at[longest] = (index_at[longest] + 1) % dims[longest]
    return values.at[tuple(index_at)].set(high)


def shard_levels(stream_key, dims, pieces, smallest, largest):
    gain, own = 1.0, jax.random.fold_in(stream_key, 6)
    for position, parts in pieces:
        draws = jnp.exp(jax.random.uniform(jax.random.fold_in(own, position), (parts,), jnp.float32, smallest / len(pieces), largest / len(pieces)))
        gain = gain * jnp.repeat(draws, dims[position] // parts).reshape([-1 if axis == position else 1 for axis in range(len(dims))])
    return gain


def normal_values(stream_key, shape, spread, bound, cuts=(), held_as=jnp.bfloat16):
    factor_of = shard_levels(stream_key, shape, cuts, -0.22, 0.18) if cuts else 1.0
    values = jax.random.normal(stream_key, shape, jnp.float32) * spread * factor_of
    return jnp.minimum(jnp.maximum(values, -bound), bound).astype(held_as)


def setup_inputs(seed: int = 0) -> dict:
    keys = jax.random.split(jax.random.key(seed), 12)
    return {
        "latents": draw_latents(jax.random.fold_in(keys[11], 71), 0),
        "known": normal_values(keys[1], (TOKENS, D), 1.0, 6.0, ((0, 128), (1, 2))),
        "seam_mask": touch_ends((jax.random.randint(keys[2], (TOKENS,), 0, 2) < 1).astype(jnp.int32), jax.random.fold_in(keys[2], 1), 0, 1),
        "timesteps": draw_timesteps(jax.random.fold_in(keys[11], 71), 0),
        "block_lists": draw_block_lists(jax.random.fold_in(keys[11], 71), 0),
        "guidance": draw_guidance(jax.random.fold_in(keys[11], 71), 0),
        "modulation_weight": normal_values(keys[6], (FREQ, 4, D), (FREQ // 4) ** -0.5, 0.75),
        "self_weight": draw_self_weight(jax.random.fold_in(keys[11], 71), 0),
        "self_out_weight": normal_values(keys[8], (D, D), D ** -0.5, 0.1875, ((0, 2),)),
        "cross_weight": draw_cross_weight(jax.random.fold_in(keys[11], 71), 0),
        "cross_out_weight": normal_values(keys[10], (D, D), D ** -0.5, 0.1875, ((0, 2),)),
    }


def widen(values):
    return lax.optimization_barrier(values).astype(jnp.float32)

def norm_rows(values):
    values = values.astype(jnp.float32)
    center = values - lax.optimization_barrier(jnp.mean(values, axis=-1, keepdims=True))
    second = lax.optimization_barrier(jnp.mean(center * center, axis=-1, keepdims=True))
    return center * lax.rsqrt(second + 1e-06)

def signal_level(moment):
    angle = (moment.astype(jnp.float32) / 1000.0 + 0.008) / 1.008 * (math.pi / 2.0)
    cosine = jnp.cos(angle)
    return cosine * cosine

def modulation_table(moment, modulation_weight):
    half = FREQ // 2
    frequency = jnp.exp(-math.log(10000.0) * jnp.arange(half, dtype=jnp.float32) / half)
    phase = moment.astype(jnp.float32) * frequency
    embed = jnp.concatenate([jnp.cos(phase), jnp.sin(phase)])
    active = jax.nn.silu(embed).astype(jnp.bfloat16)
    width = modulation_weight.shape[2]
    table = jnp.dot(active[None, :], modulation_weight.reshape(FREQ, 4 * width), preferred_element_type=jnp.float32)
    return table.reshape(4, width)

def sparse_attention(query, pair, block_lists):
    scale = 1.0 / math.sqrt(HEAD_DIM)
    query_blocks = query.reshape(NBLK, BLOCK, HEADS, HEAD_DIM)
    pair_blocks = pair.reshape(NBLK, BLOCK, 2, HEADS, HEAD_DIM)

    def one_block(operand):
        queries, entries = operand
        valid = entries >= 0
        picked = jnp.where(valid, entries, 0).astype(jnp.int32)
        chosen = pair_blocks[picked].reshape(MAXK * BLOCK, 2, HEADS, HEAD_DIM)
        scores = jnp.einsum('qhd,khd->hqk', widen(queries), widen(chosen[:, 0])) * scale
        live = jnp.repeat(valid, BLOCK)
        scores = jnp.where(live[None, None, :], scores, -1e+30)
        peak = lax.optimization_barrier(jnp.max(scores, axis=-1, keepdims=True))
        weights = jnp.exp(scores - peak)
        total = lax.optimization_barrier(jnp.sum(weights, axis=-1))
        rounded = weights.astype(jnp.bfloat16)
        mixed = jnp.einsum('hqk,khd->qhd', widen(rounded), widen(chosen[:, 1]))
        mixed = mixed / jnp.transpose(total)[:, :, None]
        return mixed.reshape(BLOCK, HEADS * HEAD_DIM).astype(jnp.bfloat16)
    result = lax.map(one_block, (query_blocks, block_lists))
    return result.reshape(NBLK * BLOCK, HEADS * HEAD_DIM)

def guided_attention(query, guide_pair):
    scale = 1.0 / math.sqrt(HEAD_DIM)
    guide_keys = widen(guide_pair[:, 0]).reshape(G, HEADS, HEAD_DIM)
    guide_values = widen(guide_pair[:, 1]).reshape(G, HEADS, HEAD_DIM)
    query_blocks = query.reshape(NBLK, BLOCK, HEADS, HEAD_DIM)

    def one_block(queries):
        scores = jnp.einsum('qhd,ghd->hqg', widen(queries), guide_keys) * scale
        peak = lax.optimization_barrier(jnp.max(scores, axis=-1, keepdims=True))
        weights = jnp.exp(scores - peak)
        total = lax.optimization_barrier(jnp.sum(weights, axis=-1))
        rounded = weights.astype(jnp.bfloat16)
        mixed = jnp.einsum('hqg,ghd->qhd', widen(rounded), guide_values)
        mixed = mixed / jnp.transpose(total)[:, :, None]
        return mixed.reshape(BLOCK, HEADS * HEAD_DIM).astype(jnp.bfloat16)
    result = lax.map(one_block, query_blocks)
    return result.reshape(NBLK * BLOCK, HEADS * HEAD_DIM)

def reference(latents, known, seam_mask, timesteps, block_lists, guidance, modulation_weight, self_weight, self_out_weight, cross_weight, cross_out_weight):
    state = latents
    self_flat = self_weight.reshape(D, 3 * D)
    cross_pair_weight = cross_weight[:, 1:3].reshape(D, 2 * D)
    cross_query_weight = cross_weight[:, 0]
    for step in range(STEPS):
        moment = timesteps[step]
        after = timesteps[step + 1]
        table = modulation_table(moment, modulation_weight)
        normed = norm_rows(state)
        mixed_in = (normed * (1.0 + table[1]) + table[0]).astype(jnp.bfloat16)
        plain = normed.astype(jnp.bfloat16)
        projected = jnp.dot(mixed_in, self_flat, preferred_element_type=jnp.float32).astype(jnp.bfloat16)
        projected = projected.reshape(TOKENS, 3, D)
        attended = sparse_attention(projected[:, 0], projected[:, 1:3], block_lists)
        guide_in = norm_rows(guidance[step]).astype(jnp.bfloat16)
        guide_pair = jnp.dot(guide_in, cross_pair_weight, preferred_element_type=jnp.float32).astype(jnp.bfloat16)
        guide_pair = guide_pair.reshape(G, 2, D)
        cross_query = jnp.dot(plain, cross_query_weight, preferred_element_type=jnp.float32).astype(jnp.bfloat16)
        guided = guided_attention(cross_query, guide_pair)
        noise_pred = table[2] * jnp.dot(attended, self_out_weight, preferred_element_type=jnp.float32)
        noise_pred = noise_pred + table[3] * jnp.dot(guided, cross_out_weight, preferred_element_type=jnp.float32)
        level_now = signal_level(moment)
        level_after = signal_level(after)
        current = state.astype(jnp.float32)
        clean = (current - jnp.sqrt(1.0 - level_now) * noise_pred) / jnp.sqrt(level_now)
        moved = jnp.sqrt(level_after) * clean + jnp.sqrt(1.0 - level_after) * noise_pred
        kept = jnp.sqrt(level_after) * known.astype(jnp.float32) + jnp.sqrt(1.0 - level_after) * latents.astype(jnp.float32)
        state = jnp.where(seam_mask[:, None] == 1, moved, kept).astype(jnp.bfloat16)
    return state
```

```python
import math

import jax
import jax.numpy as jnp
from jax import lax
from jax.sharding import PartitionSpec as P

D = 1024
HEAD_DIM = 64
FREQ = 256
BLOCK = 128
MAXK = 6
ROW = 4
STEPS = 2


def passed_along(block, axis, distance):
    devices = range(lax.axis_size(axis))
    route = [((i - distance) % len(devices), i) for i in devices]
    return lax.ppermute(block, axis, route)


def norm_rows(values):
    values = values.astype(jnp.float32)
    center = values - jnp.mean(values, axis=-1, keepdims=True)
    second = jnp.mean(center * center, axis=-1, keepdims=True)
    return center * lax.rsqrt(second + 1e-06)


def signal_level(moment):
    angle = (moment.astype(jnp.float32) / 1000.0 + 0.008) / 1.008 * (math.pi / 2.0)
    cosine = jnp.cos(angle)
    return cosine * cosine


def modulation_table(moment, modulation_weight):
    half = FREQ // 2
    frequency = jnp.exp(-math.log(10000.0) * jnp.arange(half, dtype=jnp.float32) / half)
    phase = moment.astype(jnp.float32) * frequency
    embed = jnp.concatenate([jnp.cos(phase), jnp.sin(phase)])
    active = jax.nn.silu(embed).astype(jnp.bfloat16)
    width = modulation_weight.shape[2]
    table = jnp.dot(
        active[None, :],
        modulation_weight.reshape(FREQ, 4 * width),
        preferred_element_type=jnp.float32,
    )
    return table.reshape(4, width)


def on_device(
    latents,
    known,
    seam_mask,
    timesteps,
    block_lists,
    guidance,
    modulation_weight,
    self_weight,
    self_out_weight,
    cross_weight,
    cross_out_weight,
):
    cycle_size = lax.axis_size("seq")
    position = lax.axis_index("seq")
    token_count = latents.shape[0]
    local_width = self_weight.shape[2]
    local_heads = local_width // HEAD_DIM
    block_count = token_count // BLOCK
    scale = 1.0 / math.sqrt(HEAD_DIM)
    moves = jnp.array([-ROW, -1, 0, 1, ROW], dtype=jnp.int32)
    tiles = (position + moves) % cycle_size
    names = tiles[:, None] * block_count + jnp.arange(block_count, dtype=jnp.int32)
    listed = jnp.any(block_lists[:, :, None] == names.reshape(-1), axis=1)
    live = jnp.repeat(listed, BLOCK, axis=1)
    self_flat = self_weight.reshape(D, 3 * local_width)
    cross_pair_weight = cross_weight[:, 1:3].reshape(D, 2 * local_width)
    cross_query_weight = cross_weight[:, 0]
    guide_count = guidance.shape[1]
    guide_pairs = []
    for step in range(STEPS):
        guide_in = norm_rows(guidance[step]).astype(jnp.bfloat16)
        paired = jnp.dot(guide_in, cross_pair_weight, preferred_element_type=jnp.float32).astype(
            jnp.bfloat16
        )
        guide_pairs.append(paired.reshape(guide_count, 2, local_width))
    state = latents
    for step in range(STEPS):
        moment = timesteps[step]
        after = timesteps[step + 1]
        table = modulation_table(moment, modulation_weight)
        whole = lax.all_gather(state, "head", axis=1, tiled=True)
        normed = norm_rows(whole)
        mixed_in = (normed * (1.0 + table[1]) + table[0]).astype(jnp.bfloat16)
        plain = normed.astype(jnp.bfloat16)
        projected = jnp.dot(mixed_in, self_flat, preferred_element_type=jnp.float32).astype(
            jnp.bfloat16
        )
        projected = projected.reshape(token_count, 3, local_width)
        query = projected[:, 0]
        pair = projected[:, 1:3]
        window = jnp.concatenate(
            [
                passed_along(pair, "seq", ROW),
                passed_along(pair, "seq", 1),
                pair,
                passed_along(pair, "seq", -1),
                passed_along(pair, "seq", -ROW),
            ],
            axis=0,
        )
        window = window.reshape(-1, 2, local_heads, HEAD_DIM)
        queries = query.reshape(block_count, BLOCK, local_heads, HEAD_DIM)
        scores = (
            jnp.einsum(
                "bqhd,khd->bhqk", queries, window[:, 0], preferred_element_type=jnp.float32
            )
            * scale
        )
        scores = jnp.where(live[:, None, None, :], scores, -1e30)
        peak = jnp.max(scores, axis=-1, keepdims=True)
        weights = jnp.exp(scores - peak)
        total = jnp.sum(weights, axis=-1)
        rounded = weights.astype(jnp.bfloat16)
        mixed = jnp.einsum(
            "bhqk,khd->bqhd", rounded, window[:, 1], preferred_element_type=jnp.float32
        )
        mixed = mixed / jnp.transpose(total, (0, 2, 1))[:, :, :, None]
        attended = mixed.reshape(token_count, local_width).astype(jnp.bfloat16)
        guide_pair = lax.all_gather(guide_pairs[step], "seq", axis=0, tiled=True)
        every_guide = guide_pair.shape[0]
        guide_keys = guide_pair[:, 0].reshape(every_guide, local_heads, HEAD_DIM)
        guide_values = guide_pair[:, 1].reshape(every_guide, local_heads, HEAD_DIM)
        cross_query = jnp.dot(plain, cross_query_weight, preferred_element_type=jnp.float32).astype(
            jnp.bfloat16
        )
        cross_heads = cross_query.reshape(token_count, local_heads, HEAD_DIM)
        cross_scores = (
            jnp.einsum("qhd,ghd->hqg", cross_heads, guide_keys, preferred_element_type=jnp.float32)
            * scale
        )
        cross_peak = jnp.max(cross_scores, axis=-1, keepdims=True)
        cross_weights = jnp.exp(cross_scores - cross_peak)
        cross_total = jnp.sum(cross_weights, axis=-1)
        cross_rounded = cross_weights.astype(jnp.bfloat16)
        cross_mixed = jnp.einsum(
            "hqg,ghd->qhd", cross_rounded, guide_values, preferred_element_type=jnp.float32
        )
        cross_mixed = cross_mixed / jnp.transpose(cross_total)[:, :, None]
        guided = cross_mixed.reshape(token_count, local_width).astype(jnp.bfloat16)
        partial_value = table[2] * jnp.dot(
            attended, self_out_weight, preferred_element_type=jnp.float32
        )
        partial_value = partial_value + table[3] * jnp.dot(
            guided, cross_out_weight, preferred_element_type=jnp.float32
        )
        noise_pred = lax.psum_scatter(partial_value, "head", scatter_dimension=1, tiled=True)
        level_now = signal_level(moment)
        level_after = signal_level(after)
        current = state.astype(jnp.float32)
        clean = (current - jnp.sqrt(1.0 - level_now) * noise_pred) / jnp.sqrt(level_now)
        moved = jnp.sqrt(level_after) * clean + jnp.sqrt(1.0 - level_after) * noise_pred
        kept = jnp.sqrt(level_after) * known.astype(jnp.float32) + jnp.sqrt(
            1.0 - level_after
        ) * latents.astype(jnp.float32)
        state = jnp.where(seam_mask[:, None] == 1, moved, kept).astype(jnp.bfloat16)
    return state


def solution(mesh):
    in_specs = (
        P("seq", "head"),
        P("seq", "head"),
        P("seq"),
        P(),
        P("seq", None),
        P(None, "seq", None),
        P(),
        P(None, None, "head"),
        P("head", None),
        P(None, None, "head"),
        P("head", None),
    )
    out_specs = P("seq", "head")
    return jax.shard_map(
        on_device, mesh=mesh, in_specs=in_specs, out_specs=out_specs, check_vma=False
    )
```

```python
import functools
import math

import jax
import jax.numpy as jnp
from jax import lax
from jax.experimental import pallas as pl
from jax.experimental.pallas import tpu as pltpu
from jax.sharding import PartitionSpec as P

D = 1024
HALF = 512
HEAD_DIM = 64
FREQ = 256
BLOCK = 128
TOK = 256
STEPS = 2
NSEQ = 128
GUIDE = 8
MESH = pl.DeviceIdType.MESH
F32 = jnp.float32
BF16 = jnp.bfloat16
OWN, CORE, UP, DOWN, OVER = range(5)


def signal_level(moment):
    angle = (moment.astype(F32) / 1000.0 + 0.008) / 1.008 * (math.pi / 2.0)
    cosine = jnp.cos(angle)
    return cosine * cosine


def places(s):
    q = lax.rem(s, 4)
    wrap = lambda v: lax.rem(v + NSEQ, NSEQ)
    turn = lambda d: 16 * (s // 16) + lax.rem(lax.rem(s, 16) + 4 * d, 16)
    return dict(
        core=s + 1 - 2 * lax.rem(s, 2),
        over=4 * (s // 4) + 3 - q,
        diag=4 * (s // 4) + lax.rem(q + 2, 4),
        up=wrap(s + 4),
        down=wrap(s - 4),
        turn1=turn(1),
        turn2=turn(2),
        turn3=turn(3),
        zup=wrap(s + 16),
        zdown=wrap(s - 16),
    )


def norm(parts):
    width = sum(p.shape[1] for p in parts)
    mean = sum(jnp.sum(p, axis=1, keepdims=True) for p in parts) * (1.0 / width)
    parts = [p - mean for p in parts]
    var = sum(jnp.sum(p * p, axis=1, keepdims=True) for p in parts) * (1.0 / width)
    scale = lax.rsqrt(var + 1e-06)
    return [p * scale for p in parts]


def kernel(
    active, coef, mask, bias, guid, lat, known, mw, sw, sow, cw, cow,
    out,
    latv, knownv, statev, mwv, swv, sowv, cwv, cowv, tab, mixb, plainb, kvb, gb, ab,
    qs, cqs, acc, mx, att, gud, part, psend, precv, pfin,
    lsem, hs, hr, kss, krs, kvs, kvr, gas, gar, gbs, gbr, zs, zr, cs, cr, ps, pr,
):
    s = lax.axis_index("seq")
    h = lax.axis_index("head")
    q = lax.rem(s, 4)
    c = lax.rem(s, 2)
    at = places(s)
    to = {k: {"seq": v, "head": h} for k, v in at.items()}
    to["head"] = {"seq": s, "head": 1 - h}

    loads = [
        (cw.at[1], cwv.at[1]),
        (cw.at[2], cwv.at[2]),
        (lat, latv.at[h]),
        (sw.at[1], swv.at[1]),
        (sw.at[2], swv.at[2]),
        (mw, mwv),
        (sw.at[0], swv.at[0]),
        (cw.at[0], cwv.at[0]),
        (sow, sowv),
        (cow, cowv),
        (known, knownv.at[h]),
    ]
    loads = [pltpu.make_async_copy(a, b, lsem.at[n]) for n, (a, b) in enumerate(loads)]
    for load in loads:
        load.start()

    barrier = pltpu.get_barrier_semaphore()
    for place in to.values():
        pl.semaphore_signal(barrier, inc=1, device_id=place, device_id_type=MESH)
    pl.semaphore_wait(barrier, len(to))

    def remote(src, dst, send, recv, place):
        return pltpu.make_async_remote_copy(
            src_ref=src, dst_ref=dst, send_sem=send, recv_sem=recv,
            device_id=to[place], device_id_type=MESH,
        )

    sent = []

    def send(*args):
        copy = remote(*args)
        copy.start()
        sent.append(copy)

    def rows(b):
        return pl.ds(BLOCK * b, BLOCK)

    for b in range(2):
        send(lat.at[rows(b)], latv.at[h, rows(b)], hs.at[b], hr.at[b], "head")

    loads[0].wait()
    loads[1].wait()
    guide_in = norm([guid[...].astype(F32)])[0].astype(BF16)
    for j in range(2):
        ab[q, :, HALF * j : HALF * (j + 1)] = jnp.dot(
            guide_in, cwv[j + 1], preferred_element_type=F32
        ).astype(BF16)
    for n, place in enumerate(("core", "over", "diag")):
        send(ab.at[q], ab.at[q], gas.at[n], gar.at[n], place)

    loads[5].wait()

    def modulate(k, sums):
        row = mwv[k].astype(F32)
        return sums[0] + active[0, k] * row, sums[1] + active[1, k] * row

    zero = jnp.zeros((4, D), F32)
    tab[0], tab[1] = lax.fori_loop(0, FREQ, modulate, (zero, zero), unroll=4)

    def guide_second():
        for n, place in enumerate(("core", "over", "diag")):
            remote(ab.at[q], ab.at[q], gas.at[n], gar.at[n], place).wait_recv()
        lanes = pl.ds(pl.multiple_of(HALF * c, HALF), HALF)
        own = [ab[k, :, lanes].astype(F32) for k in range(4)]
        for i in range(STEPS):
            gb[c, i, 0, 0:32, :] = jnp.concatenate(
                [o[GUIDE * i : GUIDE * (i + 1)] for o in own], axis=0
            ).astype(BF16)
            for d in range(1, 4):
                send(
                    gb.at[c, i, 0, 0:32], gb.at[c, i, 0, 32 * d : 32 * d + 32],
                    gbs.at[i, d - 1], gbr.at[i, d - 1], f"turn{d}",
                )

    def ring(i, src, dst):
        send(gb.at[c, i, src], gb.at[c, i, dst], zs.at[i, dst], zr.at[i, dst],
             "zup" if dst in (1, 3, 5) else "zdown")

    def across(i, slot):
        send(gb.at[c, i, slot], gb.at[c, i, slot], cs.at[i, slot], cr.at[i, slot], "core")

    def guide_third(i):
        for d in range(1, 4):
            remote(
                gb.at[c, i, 0, 0:32], gb.at[c, i, 0, 32 * d : 32 * d + 32],
                gbs.at[i, d - 1], gbr.at[i, d - 1], f"turn{d}",
            ).wait_recv()
        ring(i, 0, 1)
        ring(i, 0, 2)
        across(i, 0)

    onward = {1: 3, 2: 4, 3: 5, 4: 6, 6: 7}

    def hop(i, *slots):
        for slot in slots:
            remote(gb.at[c, i, 0], gb.at[c, i, slot], zs.at[i, slot], zr.at[i, slot],
                   "zup").wait_recv()
            if slot in onward:
                ring(i, slot, onward[slot])
            across(i, slot)

    lane = lax.broadcasted_iota(jnp.int32, (1, BLOCK), 1)
    low = jnp.where(lane < HEAD_DIM, 1.0, 0.0).astype(BF16)
    low_f = lax.broadcasted_iota(jnp.int32, (TOK, BLOCK), 1) < HEAD_DIM
    high = (1.0 - low.astype(F32)).astype(BF16)

    def normalize(b, state):
        r = rows(b)
        normed = norm([state[0, r].astype(F32), state[1, r].astype(F32)])
        return r, normed

    def mix(i, b, state):
        r, normed = normalize(b, state)
        for n in range(2):
            cols = slice(HALF * n, HALF * (n + 1))
            mixb[r, cols] = (normed[n] * (1.0 + tab[i, 1:2, cols]) + tab[i, 0:1, cols]).astype(BF16)
            plainb[r, cols] = normed[n].astype(BF16)

    def keys_values(i, b):
        r = rows(b)
        x = mixb[r, :]
        for j in range(2):

            def tile(t, _):
                w = swv[1 + j, :, pl.ds(pl.multiple_of(256 * t, 256), 256)]
                kvb[i, OWN, r, pl.ds(pl.multiple_of(HALF * j + 256 * t, 256), 256)] = jnp.dot(
                    x, w, preferred_element_type=F32
                ).astype(BF16)
                return 0

            lax.fori_loop(0, 2, tile, 0)
        for n, (slot, place) in enumerate(((CORE, "core"), (DOWN, "up"), (UP, "down"))):
            send(kvb.at[i, OWN, r], kvb.at[i, slot, r], kvs.at[i, n, b], kvr.at[i, slot, b], place)

        @pl.when(q * (3 - q) > 0)
        def _():
            remote(kvb.at[i, OWN, r], kvb.at[i, OVER, r], kvs.at[i, 3, b], kvr.at[i, OVER, b], "over").start()

        sent.append(remote(kvb.at[i, OWN, r], kvb.at[i, OVER, r], kvs.at[i, 3, b], kvr.at[i, OVER, b], "over"))

    def arrived(i, slot, b):
        remote(kvb.at[i, OWN, rows(b)], kvb.at[i, slot, rows(b)], kvs.at[i, 0, b],
               kvr.at[i, slot, b], "core").wait_recv()

    def relay(i, b):
        arrived(i, UP, b)
        arrived(i, DOWN, b)
        r = rows(b)

        @pl.when(q * (3 - q) == 0)
        def _():
            remote(kvb.at[i, UP + q // 3, r], kvb.at[i, OVER, r], kvs.at[i, 3, b], kvr.at[i, OVER, b], "over").start()

    row_id = lax.broadcasted_iota(jnp.int32, (TOK, BLOCK), 0) // BLOCK
    lane_id = lax.broadcasted_iota(jnp.int32, (TOK, BLOCK), 1)

    def queries(x_ref, w_ref, dst, marked):
        def tile(t, _):
            w = w_ref[0, :, pl.ds(pl.multiple_of(256 * t, 256), 256)]
            y = jnp.dot(x_ref[...], w, preferred_element_type=F32)
            y = y.astype(BF16).astype(F32) * (1.0 / math.sqrt(HEAD_DIM))
            for u in range(2):
                z = y[:, BLOCK * u : BLOCK * (u + 1)]
                mark_a = jnp.where(lane_id == HEAD_DIM + row_id, 1.0, 0.0) if marked else 0.0
                mark_b = jnp.where(lane_id == row_id, 1.0, 0.0) if marked else 0.0
                dst[4 * t + 2 * u] = jnp.where(low_f, z, mark_a).astype(BF16)
                dst[4 * t + 2 * u + 1] = jnp.where(low_f, mark_b, z).astype(BF16)
            return 0

        lax.fori_loop(0, 2, tile, 0)

    def attend(q_ref, load, first, marks=None):
        keep = (low, high)

        def pair(p, _):
            k, v = load(pl.ds(pl.multiple_of(BLOCK * p, BLOCK), BLOCK))
            for u in range(2):
                head = 2 * p + u
                ku = k if marks is None else k * keep[u] + marks[u]
                vu = v * keep[u] + keep[1 - u]
                scores = lax.dot_general(
                    q_ref[head], ku, (((1,), (1,)), ((), ())), preferred_element_type=F32
                )
                peak = jnp.max(scores, axis=1, keepdims=True)
                if not first:
                    old = mx[head]
                    peak = jnp.maximum(peak, old[:, 0:1])
                weights = jnp.exp(scores - peak).astype(BF16)
                mixed = jnp.dot(weights, vu, preferred_element_type=F32)
                wide = jnp.broadcast_to(peak, (TOK, BLOCK))
                if not first:
                    mixed = mixed + acc[head] * jnp.exp(old - wide)
                acc[head] = mixed
                mx[head] = wide
            return 0

        lax.fori_loop(0, 4, pair, 0)

    def attend_tile(i, slot):
        marks = [
            jnp.concatenate(
                [jnp.broadcast_to(bias[u, 2 * slot + b : 2 * slot + b + 1, :], (BLOCK, BLOCK)) for b in range(2)],
                axis=0,
            ).astype(BF16)
            for u in range(2)
        ]

        def load(lanes):
            return kvb[i, slot, :, lanes], kvb[i, slot, :, pl.ds(HALF + lanes.start, BLOCK)]

        attend(qs, load, slot == OWN, marks)

    def attend_guide(i, n):
        def load(lanes):
            return [
                gb[j, i, 2 * n : 2 * n + 2, :, lanes].reshape(TOK, BLOCK) for j in range(2)
            ]

        attend(cqs, load, n == 0)

    def crossed(i, *slots):
        for slot in slots:
            remote(gb.at[c, i, 0], gb.at[1 - c, i, slot], cs.at[i, slot], cr.at[i, slot],
                   "core").wait_recv()

    def finish(dst):
        def pair(p, _):
            a, b = acc[2 * p], acc[2 * p + 1]
            a = a / pltpu.roll(a, HEAD_DIM, 1)
            b = b / pltpu.roll(b, HEAD_DIM, 1)
            dst[:, pl.ds(pl.multiple_of(BLOCK * p, BLOCK), BLOCK)] = jnp.where(low_f, a, b).astype(BF16)
            return 0

        lax.fori_loop(0, 4, pair, 0)

    def project(i, b, x_ref, w_ref, gate, first):
        r = rows(b)
        x = x_ref[r, :]

        def tile(t, _):
            cols = pl.ds(pl.multiple_of(256 * t, 256), 256)
            y = jnp.dot(x, w_ref[:, cols], preferred_element_type=F32) * tab[i, gate : gate + 1, cols]
            y = y if first else y + part[r, cols]
            part[r, cols] = y
            if not first:
                psend[i, r, cols] = y.astype(BF16)
            return 0

        lax.fori_loop(0, 4, tile, 0)

    def seam(b):
        flags = jnp.broadcast_to(mask[b : b + 1, :], (BLOCK, BLOCK))
        wide = jnp.transpose(flags)
        return jnp.concatenate([wide] * 4, axis=1) > 0.5

    def updated(i, b, n, state, noise):
        r = rows(b)
        moved = coef[4 * i] * state + coef[4 * i + 1] * noise
        kept = coef[4 * i + 2] * knownv[n, r].astype(F32) + coef[4 * i + 3] * latv[n, r].astype(F32)
        return jnp.where(seam(b), moved, kept).astype(BF16)

    loads[2].wait()
    loads[3].wait()
    loads[4].wait()
    for b in range(2):
        remote(lat.at[rows(b)], latv.at[1 - h, rows(b)], hs.at[b], hr.at[b], "head").wait_recv()
        mix(0, b, latv)
        keys_values(0, b)
        if b == 0:
            guide_second()
    loads[6].wait()
    loads[7].wait()
    send(known, knownv.at[h], kss.at[0], krs.at[0], "head")
    queries(mixb, swv, qs, True)
    queries(plainb, cwv, cqs, False)
    guide_third(0)
    guide_third(1)
    attend_tile(0, OWN)
    hop(0, 1, 2)
    relay(0, 0)
    arrived(0, CORE, 0)
    arrived(0, CORE, 1)
    attend_tile(0, CORE)
    hop(1, 1, 2)
    hop(0, 3, 4)
    relay(0, 1)
    attend_tile(0, UP)
    hop(0, 5, 6)
    hop(1, 3, 4)
    attend_tile(0, DOWN)
    hop(0, 7)
    hop(1, 5, 6)
    arrived(0, OVER, 0)
    arrived(0, OVER, 1)
    attend_tile(0, OVER)
    hop(1, 7)
    finish(att)
    for n in range(4):
        crossed(0, 2 * n, 2 * n + 1)
        attend_guide(0, n)
    finish(gud)
    loads[8].wait()
    loads[9].wait()
    for b in range(2):
        project(0, b, att, sowv, 2, True)
        project(0, b, gud, cowv, 3, False)
        send(psend.at[0, rows(b)], precv.at[rows(b)], ps.at[0, b], pr.at[0, b], "head")

    loads[10].wait()
    remote(known, knownv.at[1 - h], kss.at[0], krs.at[0], "head").wait_recv()
    for b in range(2):
        r = rows(b)
        remote(psend.at[0, r], precv.at[r], ps.at[0, b], pr.at[0, b], "head").wait_recv()
        for n in range(2):
            cols = slice(HALF * n, HALF * (n + 1))
            noise = part[r, cols] + precv[r, cols].astype(F32)
            statev[n, r] = updated(0, b, n, latv[n, r].astype(F32), noise)
        mix(1, b, statev)
        keys_values(1, b)
    queries(plainb, cwv, cqs, False)
    queries(mixb, swv, qs, True)
    crossed(1, *range(8))
    attend_guide(1, 0)
    attend_guide(1, 1)
    relay(1, 0)
    attend_guide(1, 2)
    attend_guide(1, 3)
    relay(1, 1)
    finish(gud)
    for b in range(2):
        project(1, b, gud, cowv, 3, True)
    attend_tile(1, OWN)
    arrived(1, CORE, 0)
    arrived(1, CORE, 1)
    attend_tile(1, CORE)
    attend_tile(1, UP)
    attend_tile(1, DOWN)
    arrived(1, OVER, 0)
    arrived(1, OVER, 1)
    attend_tile(1, OVER)
    finish(att)
    mine = pl.ds(pl.multiple_of(HALF * h, HALF), HALF)
    theirs = pl.ds(pl.multiple_of(HALF * (1 - h), HALF), HALF)
    for b in range(2):
        project(1, b, att, sowv, 2, False)
        send(psend.at[1, rows(b), theirs], pfin.at[rows(b)], ps.at[1, b], pr.at[1, b], "head")
    for b in range(2):
        r = rows(b)
        remote(psend.at[1, r, theirs], pfin.at[r], ps.at[1, b], pr.at[1, b], "head").wait_recv()
        noise = part[r, mine] + pfin[r].astype(F32)
        out[r] = updated(1, b, h, statev[h, r].astype(F32), noise)

    for copy in sent:
        copy.wait_send()


def on_device(
    latents, known, seam_mask, timesteps, block_lists, guidance,
    modulation_weight, self_weight, self_out_weight, cross_weight, cross_out_weight,
):
    s = lax.axis_index("seq")
    at = places(s)
    other = 2 * s - at["core"]
    names = jnp.stack([s, at["core"], at["up"], at["down"], lax.rem(other + NSEQ, NSEQ)])
    names = (2 * names[:, None] + jnp.arange(2)).reshape(-1)
    listed = jnp.any(block_lists[:, :, None] == names, axis=1)
    shut = jnp.where(listed, 0.0, -1e30).astype(F32)
    lanes = jnp.arange(BLOCK)
    bias = jnp.stack(
        [
            sum(jnp.where(lanes == base + b, shut[b][:, None], 0.0) for b in range(2))
            for base in (HEAD_DIM, 0)
        ]
    )
    half = FREQ // 2
    frequency = jnp.exp(-math.log(10000.0) * jnp.arange(half, dtype=F32) / half)
    phase = timesteps[:STEPS].astype(F32)[:, None] * frequency
    embed = jnp.concatenate([jnp.cos(phase), jnp.sin(phase)], axis=1)
    active = jax.nn.silu(embed).astype(BF16).astype(F32)
    level = signal_level(timesteps)
    root, rest = jnp.sqrt(level), jnp.sqrt(1.0 - level)
    ratio = root[1:] / root[:-1]
    coef = jnp.stack([ratio, rest[1:] - ratio * rest[:-1], root[1:], rest[1:]], axis=1)
    mask = seam_mask.astype(F32).reshape(2, BLOCK)
    vmem = pl.BlockSpec(memory_space=pltpu.VMEM)
    smem = pl.BlockSpec(memory_space=pltpu.SMEM)
    hbm = pl.BlockSpec(memory_space=pl.ANY)
    dma = lambda *shape: pltpu.SemaphoreType.DMA(shape)
    return pl.pallas_call(
        kernel,
        out_shape=jax.ShapeDtypeStruct((TOK, HALF), BF16),
        in_specs=[smem, smem, vmem, vmem, vmem] + [hbm] * 7,
        out_specs=vmem,
        scratch_shapes=[
            pltpu.VMEM((2, TOK, HALF), BF16),
            pltpu.VMEM((2, TOK, HALF), BF16),
            pltpu.VMEM((2, TOK, HALF), BF16),
            pltpu.VMEM((FREQ, 4, D), BF16),
            pltpu.VMEM((3, D, HALF), BF16),
            pltpu.VMEM((HALF, D), BF16),
            pltpu.VMEM((3, D, HALF), BF16),
            pltpu.VMEM((HALF, D), BF16),
            pltpu.VMEM((STEPS, 4, D), F32),
            pltpu.VMEM((TOK, D), BF16),
            pltpu.VMEM((TOK, D), BF16),
            pltpu.VMEM((STEPS, 5, TOK, D), BF16),
            pltpu.VMEM((2, STEPS, 8, BLOCK, HALF), BF16),
            pltpu.VMEM((4, STEPS * GUIDE, D), BF16),
            pltpu.VMEM((8, TOK, BLOCK), BF16),
            pltpu.VMEM((8, TOK, BLOCK), BF16),
            pltpu.VMEM((8, TOK, BLOCK), F32),
            pltpu.VMEM((8, TOK, BLOCK), F32),
            pltpu.VMEM((TOK, HALF), BF16),
            pltpu.VMEM((TOK, HALF), BF16),
            pltpu.VMEM((TOK, D), F32),
            pltpu.VMEM((STEPS, TOK, D), BF16),
            pltpu.VMEM((TOK, D), BF16),
            pltpu.VMEM((TOK, HALF), BF16),
            dma(11), dma(2), dma(2), dma(1), dma(1),
            dma(STEPS, 4, 2), dma(STEPS, 5, 2),
            dma(3), dma(3), dma(STEPS, 3), dma(STEPS, 3),
            dma(STEPS, 8), dma(STEPS, 8), dma(STEPS, 8), dma(STEPS, 8),
            dma(STEPS, 2), dma(STEPS, 2),
        ],
        compiler_params=pltpu.CompilerParams(
            collective_id=0, has_side_effects=True, vmem_limit_bytes=56 << 20
        ),
        name="denoise",
    )(
        active, coef.reshape(-1), mask, bias, guidance.reshape(STEPS * GUIDE, D),
        latents, known, modulation_weight, jnp.transpose(self_weight, (1, 0, 2)),
        self_out_weight, jnp.transpose(cross_weight, (1, 0, 2)), cross_out_weight,
    )


def solution(mesh):
    in_specs = (
        P("seq", "head"), P("seq", "head"), P("seq"), P(), P("seq", None), P(None, "seq", None),
        P(), P(None, None, "head"), P("head", None), P(None, None, "head"), P("head", None),
    )
    return jax.shard_map(
        on_device, mesh=mesh, in_specs=in_specs, out_specs=P("seq", "head"), check_vma=False
    )
```

```python
import functools
import math

import jax
import jax.numpy as jnp
from jax import lax
from jax.experimental import pallas as pl
from jax.experimental.pallas import tpu as pltpu
from jax.sharding import PartitionSpec as P

D = 1024
HALF = 512
HEAD_DIM = 64
FREQ = 256
BLOCK = 128
TOK = 256
STEPS = 2
NSEQ = 128
GUIDE = 8
MESH = pl.DeviceIdType.MESH
F32 = jnp.float32
BF16 = jnp.bfloat16
OWN, CORE, UP, DOWN, OVER = range(5)


def places(s):
    q = lax.rem(s, 4)
    wrap = lambda v: lax.rem(v + NSEQ, NSEQ)
    turn = lambda d: 16 * (s // 16) + lax.rem(lax.rem(s, 16) + 4 * d, 16)
    return dict(
        core=s + 1 - 2 * lax.rem(s, 2),
        over=4 * (s // 4) + 3 - q,
        diag=4 * (s // 4) + lax.rem(q + 2, 4),
        up=wrap(s + 4),
        down=wrap(s - 4),
        turn1=turn(1),
        turn2=turn(2),
        turn3=turn(3),
        zup=wrap(s + 16),
        zdown=wrap(s - 16),
    )


def norm(parts):
    width = sum(p.shape[1] for p in parts)
    mean = sum(jnp.sum(p, axis=1, keepdims=True) for p in parts) * (1.0 / width)
    parts = [p - mean for p in parts]
    var = sum(jnp.sum(p * p, axis=1, keepdims=True) for p in parts) * (1.0 / width)
    scale = lax.rsqrt(var + 1e-06)
    return [p * scale for p in parts]


def kernel(
    steps, lists, mask, guid, lat, known, mw, sw, sow, cw, cow,
    out,
    latv, knownv, statev, mwv, swv, sowv, cwv, cowv, acol, bias, tab, mixb, plainb, kvb, gb, gp, ab,
    qs, cqs, acc, mx, acc2, mx2, att, gud, part, psend, precv, pfin,
    lsem, hs, hr, kss, krs, kvs, kvr, gas, gar, gbs, gbr, zs, zr, cs, cr, ps, pr,
):
    s = lax.axis_index("seq")
    h = lax.axis_index("head")
    q = lax.rem(s, 4)
    c = lax.rem(s, 2)
    at = places(s)
    to = {k: {"seq": v, "head": h} for k, v in at.items()}
    to["head"] = {"seq": s, "head": 1 - h}

    loads = [
        (cw.at[1], cwv.at[1]),
        (cw.at[2], cwv.at[2]),
        (lat, latv.at[h]),
        (sw.at[1], swv.at[1]),
        (sw.at[2], swv.at[2]),
        (mw, mwv),
        (sw.at[0], swv.at[0]),
        (cw.at[0], cwv.at[0]),
        (sow, sowv),
        (cow, cowv),
        (known, knownv.at[h]),
    ]
    loads = [pltpu.make_async_copy(a, b, lsem.at[n]) for n, (a, b) in enumerate(loads)]
    for load in loads:
        load.start()

    barrier = pltpu.get_barrier_semaphore()
    for place in to.values():
        pl.semaphore_signal(barrier, inc=1, device_id=place, device_id_type=MESH)
    pl.semaphore_wait(barrier, len(to))

    def remote(src, dst, send, recv, place):
        return pltpu.make_async_remote_copy(
            src_ref=src, dst_ref=dst, send_sem=send, recv_sem=recv,
            device_id=to[place], device_id_type=MESH,
        )

    sent = []

    def send(*args):
        copy = remote(*args)
        copy.start()
        sent.append(copy)

    def rows(b):
        return pl.ds(BLOCK * b, BLOCK)

    for b in range(2):
        send(lat.at[rows(b)], latv.at[h, rows(b)], hs.at[b], hr.at[b], "head")

    loads[0].wait()
    loads[1].wait()
    guide_in = norm([guid[...].astype(F32)])[0].astype(BF16)
    for j in range(2):
        ab[q, :, HALF * j : HALF * (j + 1)] = jnp.dot(
            guide_in, cwv[j + 1], preferred_element_type=F32
        ).astype(BF16)
    for n, place in enumerate(("core", "over", "diag")):
        send(ab.at[q], ab.at[q], gas.at[n], gar.at[n], place)

    lane = lax.broadcasted_iota(jnp.int32, (1, BLOCK), 1)
    other = lax.rem(2 * s - at["core"] + NSEQ, NSEQ)
    for n, name in enumerate((s, at["core"], at["up"], at["down"], other)):
        for kb in range(2):
            shut = []
            for b in range(2):
                hit = jnp.int32(0)
                for m in range(6):
                    hit = hit | jnp.where(lists[b, m] == 2 * name + kb, 1, 0)
                shut.append(jnp.where(hit == 1, 0.0, -1e30))
            for u, base in enumerate((HEAD_DIM, 0)):
                line = jnp.where(lane == base, shut[0], jnp.where(lane == base + 1, shut[1], 0.0))
                bias[u, 2 * n + kb : 2 * n + kb + 1, :] = line

    step_row = lax.broadcasted_iota(jnp.int32, (8, BLOCK), 0)
    moment = jnp.where(
        step_row == 0, steps[0].astype(F32), jnp.where(step_row == 1, steps[1].astype(F32), steps[2].astype(F32))
    )
    which = lax.broadcasted_iota(jnp.int32, (8, BLOCK), 1).astype(F32)
    phase = moment * jnp.exp(which * (-math.log(10000.0) / (FREQ // 2)))
    for n, embed in enumerate((jnp.cos(phase), jnp.sin(phase))):
        embed = (embed / (1.0 + jnp.exp(-embed))).astype(BF16).astype(F32)
        for i in range(STEPS):
            acol[i, BLOCK * n : BLOCK * (n + 1), :] = jnp.transpose(
                jnp.broadcast_to(embed[i : i + 1, :], (BLOCK, BLOCK))
            )
    cosine = jnp.cos((moment / 1000.0 + 0.008) / 1.008 * (math.pi / 2.0))
    level = cosine * cosine
    root, rest = jnp.sqrt(level), jnp.sqrt(1.0 - level)
    coefs = []
    for i in range(STEPS):
        ratio = root[i + 1 : i + 2] / root[i : i + 1]
        line = (ratio, rest[i + 1 : i + 2] - ratio * rest[i : i + 1], root[i + 1 : i + 2], rest[i + 1 : i + 2])
        coefs.append([jnp.concatenate([x] * 4, axis=1) for x in line])

    loads[5].wait()

    def modulate(k, sums):
        row = mwv[k].astype(F32)
        scale = [jnp.concatenate([acol[i, pl.ds(k, 1), :]] * 8, axis=1) for i in range(STEPS)]
        return sums[0] + scale[0] * row, sums[1] + scale[1] * row

    zero = jnp.zeros((4, D), F32)
    tab[0], tab[1] = lax.fori_loop(0, FREQ, modulate, (zero, zero), unroll=4)

    def guide_second():
        for n, place in enumerate(("core", "over", "diag")):
            remote(ab.at[q], ab.at[q], gas.at[n], gar.at[n], place).wait_recv()
        lanes = pl.ds(pl.multiple_of(HALF * c, HALF), HALF)
        own = [ab[k, :, lanes].astype(F32) for k in range(4)]
        for i in range(STEPS):
            gp[i, 0:32, :] = jnp.concatenate(
                [o[GUIDE * i : GUIDE * (i + 1)] for o in own], axis=0
            ).astype(BF16)
            for d in range(1, 4):
                send(
                    gp.at[i, 0:32], gp.at[i, 32 * d : 32 * d + 32],
                    gbs.at[i, d - 1], gbr.at[i, d - 1], f"turn{d}",
                )

    def ring(i, src, dst):
        send(gb.at[c, i, src], gb.at[c, i, dst], zs.at[i, dst], zr.at[i, dst],
             "zup" if dst in (1, 3, 5) else "zdown")

    def across(i, slot):
        send(gb.at[c, i, slot], gb.at[c, i, slot], cs.at[i, slot], cr.at[i, slot], "core")

    def guide_third(i):
        for d in range(1, 4):
            remote(
                gp.at[i, 0:32], gp.at[i, 32 * d : 32 * d + 32],
                gbs.at[i, d - 1], gbr.at[i, d - 1], f"turn{d}",
            ).wait_recv()
        for p in range(4):
            cols = slice(BLOCK * p, BLOCK * (p + 1))
            y = gp[i, :, cols].astype(F32)
            gb[c, i, 0, :, cols] = jnp.where(c == 1, jnp.transpose(y), y).astype(BF16)
        ring(i, 0, 1)
        ring(i, 0, 2)
        across(i, 0)

    onward = {1: 3, 2: 4, 3: 5, 4: 6, 6: 7}

    def hop(i, *slots):
        for slot in slots:
            remote(gb.at[c, i, 0], gb.at[c, i, slot], zs.at[i, slot], zr.at[i, slot],
                   "zup").wait_recv()
            if slot in onward:
                ring(i, slot, onward[slot])
            across(i, slot)

    lane = lax.broadcasted_iota(jnp.int32, (1, BLOCK), 1)
    low = jnp.where(lane < HEAD_DIM, 1.0, 0.0).astype(BF16)
    low_f = lax.broadcasted_iota(jnp.int32, (TOK, BLOCK), 1) < HEAD_DIM
    keep = (low, (1.0 - low.astype(F32)).astype(BF16))

    def normalize(b, state):
        r = rows(b)
        normed = norm([state[0, r].astype(F32), state[1, r].astype(F32)])
        return r, normed

    def mix(i, b, state):
        r, normed = normalize(b, state)
        for n in range(2):
            cols = slice(HALF * n, HALF * (n + 1))
            mixb[r, cols] = (normed[n] * (1.0 + tab[i, 1:2, cols]) + tab[i, 0:1, cols]).astype(BF16)
            plainb[r, cols] = normed[n].astype(BF16)

    def keys_values(i, b):
        r = rows(b)
        x = mixb[r, :]
        for j in range(2):

            def tile(t, _):
                w = swv[1 + j, :, pl.ds(pl.multiple_of(256 * t, 256), 256)]
                y = jnp.dot(x, w, preferred_element_type=F32)
                if j == 1:
                    y = jnp.concatenate(
                        [jnp.transpose(y[:, BLOCK * u : BLOCK * (u + 1)]) for u in range(2)], axis=1
                    )
                cols = pl.ds(pl.multiple_of(HALF * j + 256 * t, 256), 256)
                kvb[i, OWN, r, cols] = y.astype(BF16)
                return 0

            lax.fori_loop(0, 2, tile, 0)
        for n, (slot, place) in enumerate(((CORE, "core"), (DOWN, "up"), (UP, "down"))):
            send(kvb.at[i, OWN, r], kvb.at[i, slot, r], kvs.at[i, n, b], kvr.at[i, slot, b], place)

        @pl.when(q * (3 - q) > 0)
        def _():
            remote(kvb.at[i, OWN, r], kvb.at[i, OVER, r], kvs.at[i, 3, b], kvr.at[i, OVER, b], "over").start()

        sent.append(remote(kvb.at[i, OWN, r], kvb.at[i, OVER, r], kvs.at[i, 3, b], kvr.at[i, OVER, b], "over"))

    def arrived(i, slot, b):
        remote(kvb.at[i, OWN, rows(b)], kvb.at[i, slot, rows(b)], kvs.at[i, 0, b],
               kvr.at[i, slot, b], "core").wait_recv()

    def relay(i, b):
        arrived(i, UP, b)
        arrived(i, DOWN, b)
        r = rows(b)

        @pl.when(q * (3 - q) == 0)
        def _():
            remote(kvb.at[i, UP + q // 3, r], kvb.at[i, OVER, r], kvs.at[i, 3, b], kvr.at[i, OVER, b], "over").start()

    row_id = lax.broadcasted_iota(jnp.int32, (TOK, BLOCK), 0) // BLOCK
    lane_id = lax.broadcasted_iota(jnp.int32, (TOK, BLOCK), 1)

    def queries(x_ref, w_ref, dst, marked):
        def tile(t, _):
            w = w_ref[0, :, pl.ds(pl.multiple_of(256 * t, 256), 256)]
            y = jnp.dot(x_ref[...], w, preferred_element_type=F32)
            y = y.astype(BF16).astype(F32) * (1.0 / math.sqrt(HEAD_DIM))
            for u in range(2):
                z = y[:, BLOCK * u : BLOCK * (u + 1)]
                mark_a = jnp.where(lane_id == HEAD_DIM + row_id, 1.0, 0.0) if marked else 0.0
                mark_b = jnp.where(lane_id == row_id, 1.0, 0.0) if marked else 0.0
                dst[4 * t + 2 * u] = jnp.where(low_f, z, mark_a).astype(BF16)
                dst[4 * t + 2 * u + 1] = jnp.where(low_f, mark_b, z).astype(BF16)
            return 0

        lax.fori_loop(0, 2, tile, 0)

    ones = jnp.ones((16, TOK), BF16)

    def attend(q_ref, tiles, first, sums, peaks):
        def pair(p, _):
            lanes = pl.ds(pl.multiple_of(BLOCK * p, BLOCK), BLOCK)
            loaded = [load(lanes) for load, _ in tiles]
            for u in range(2):
                head = 2 * p + u
                scores = []
                for (k, _), (_, marks) in zip(loaded, tiles):
                    k = k if marks is None else k * keep[u] + marks[u]
                    scores.append(
                        lax.dot_general(
                            k, q_ref[head], (((1,), (1,)), ((), ())), preferred_element_type=F32
                        )
                    )
                peak = functools.reduce(
                    jnp.maximum, [jnp.max(x, axis=0, keepdims=True) for x in scores]
                )
                if not first:
                    old = peaks[head, 0:1, :]
                    peak = jnp.maximum(peak, old)
                mixed = None
                for x, (_, v) in zip(scores, loaded):
                    v = jnp.concatenate([v[HEAD_DIM * u : HEAD_DIM * (u + 1)], ones], axis=0)
                    y = jnp.dot(v, jnp.exp(x - peak).astype(BF16), preferred_element_type=F32)
                    mixed = y if mixed is None else mixed + y
                if not first:
                    mixed = mixed + sums[head] * jnp.exp(old - peak)
                sums[head] = mixed
                peaks[head, 0:1, :] = peak
            return 0

        lax.fori_loop(0, 4, pair, 0)

    def attend_tiles(i, *slots):
        def tile(slot):
            marks = [
                jnp.concatenate(
                    [
                        jnp.broadcast_to(
                            bias[u, 2 * slot + b : 2 * slot + b + 1, :], (BLOCK, BLOCK)
                        )
                        for b in range(2)
                    ],
                    axis=0,
                ).astype(BF16)
                for u in range(2)
            ]

            def load(lanes):
                high_lanes = pl.ds(HALF + lanes.start, BLOCK)
                v = [kvb[i, slot, BLOCK * b : BLOCK * (b + 1), high_lanes] for b in range(2)]
                return kvb[i, slot, :, lanes], jnp.concatenate(v, axis=1)

            return load, marks

        attend(qs, [tile(slot) for slot in slots], slots[0] == OWN, acc, mx)

    def attend_guide(i, *chunks):
        def tile(n):
            def load(lanes):
                k = gb[0, i, 2 * n : 2 * n + 2, :, lanes].reshape(TOK, BLOCK)
                v = [gb[1, i, 2 * n + b, :, lanes] for b in range(2)]
                return k, jnp.concatenate(v, axis=1)

            return load, None

        attend(cqs, [tile(n) for n in chunks], chunks[0] == 0, acc2, mx2)

    def crossed(i, *slots):
        for slot in slots:
            remote(gb.at[c, i, 0], gb.at[1 - c, i, slot], cs.at[i, slot], cr.at[i, slot],
                   "core").wait_recv()

    def finish(dst, sums):
        def pair(p, _):
            y = [
                sums[2 * p + u, 0:HEAD_DIM, :] / sums[2 * p + u, HEAD_DIM : HEAD_DIM + 1, :]
                for u in range(2)
            ]
            y = jnp.concatenate(y, axis=0)
            for b in range(2):
                dst[rows(b), pl.ds(pl.multiple_of(BLOCK * p, BLOCK), BLOCK)] = jnp.transpose(
                    y[:, BLOCK * b : BLOCK * (b + 1)]
                ).astype(BF16)
            return 0

        lax.fori_loop(0, 4, pair, 0)

    def project(i, b, x_ref, w_ref, gate, first):
        r = rows(b)
        x = x_ref[r, :]

        def tile(t, _):
            cols = pl.ds(pl.multiple_of(256 * t, 256), 256)
            y = jnp.dot(x, w_ref[:, cols], preferred_element_type=F32) * tab[i, gate : gate + 1, cols]
            y = y if first else y + part[r, cols]
            part[r, cols] = y
            if not first:
                psend[i, r, cols] = y.astype(BF16)
            return 0

        lax.fori_loop(0, 4, tile, 0)

    def seam(b):
        flags = jnp.broadcast_to(mask[b : b + 1, :].astype(F32), (BLOCK, BLOCK))
        wide = jnp.transpose(flags)
        return jnp.concatenate([wide] * 4, axis=1) > 0.5

    def updated(i, b, n, state, noise):
        r = rows(b)
        moved = coefs[i][0] * state + coefs[i][1] * noise
        kept = coefs[i][2] * knownv[n, r].astype(F32) + coefs[i][3] * latv[n, r].astype(F32)
        return jnp.where(seam(b), moved, kept).astype(BF16)

    loads[2].wait()
    loads[3].wait()
    loads[4].wait()
    for b in range(2):
        remote(lat.at[rows(b)], latv.at[1 - h, rows(b)], hs.at[b], hr.at[b], "head").wait_recv()
        mix(0, b, latv)
        keys_values(0, b)
        if b == 0:
            guide_second()
    loads[6].wait()
    loads[7].wait()
    send(known, knownv.at[h], kss.at[0], krs.at[0], "head")
    queries(mixb, swv, qs, True)
    guide_third(0)
    attend_tiles(0, OWN)
    hop(0, 1, 2)
    relay(0, 0)
    queries(plainb, cwv, cqs, False)
    arrived(0, CORE, 0)
    arrived(0, CORE, 1)
    attend_tiles(0, CORE)
    hop(0, 3, 4)
    relay(0, 1)
    attend_tiles(0, UP, DOWN)
    hop(0, 5, 6)
    crossed(0, 0, 1)
    attend_guide(0, 0)
    hop(0, 7)
    guide_third(1)
    arrived(0, OVER, 0)
    arrived(0, OVER, 1)
    attend_tiles(0, OVER)
    finish(att, acc)
    loads[8].wait()
    loads[9].wait()
    for b in range(2):
        project(0, b, att, sowv, 2, True)
    crossed(0, 2, 3)
    attend_guide(0, 1)
    hop(1, 1, 2)
    crossed(0, 4, 5, 6, 7)
    attend_guide(0, 2, 3)
    finish(gud, acc2)
    for b in range(2):
        project(0, b, gud, cowv, 3, False)
        send(psend.at[0, rows(b)], precv.at[rows(b)], ps.at[0, b], pr.at[0, b], "head")
    hop(1, 3, 4)

    loads[10].wait()
    remote(known, knownv.at[1 - h], kss.at[0], krs.at[0], "head").wait_recv()
    for b in range(2):
        r = rows(b)
        remote(psend.at[0, r], precv.at[r], ps.at[0, b], pr.at[0, b], "head").wait_recv()
        for n in range(2):
            cols = slice(HALF * n, HALF * (n + 1))
            noise = part[r, cols] + precv[r, cols].astype(F32)
            statev[n, r] = updated(0, b, n, latv[n, r].astype(F32), noise)
        mix(1, b, statev)
        keys_values(1, b)
        if b == 0:
            hop(1, 5, 6)
    hop(1, 7)
    queries(mixb, swv, qs, True)
    attend_tiles(1, OWN)
    queries(plainb, cwv, cqs, False)
    relay(1, 0)
    crossed(1, *range(8))
    attend_guide(1, 0, 1)
    relay(1, 1)
    attend_guide(1, 2, 3)
    arrived(1, CORE, 0)
    arrived(1, CORE, 1)
    attend_tiles(1, CORE)
    finish(gud, acc2)
    for b in range(2):
        project(1, b, gud, cowv, 3, True)
    attend_tiles(1, UP, DOWN)
    arrived(1, OVER, 0)
    arrived(1, OVER, 1)
    attend_tiles(1, OVER)
    finish(att, acc)
    mine = pl.ds(pl.multiple_of(HALF * h, HALF), HALF)
    theirs = pl.ds(pl.multiple_of(HALF * (1 - h), HALF), HALF)
    for b in range(2):
        project(1, b, att, sowv, 2, False)
        send(psend.at[1, rows(b), theirs], pfin.at[rows(b)], ps.at[1, b], pr.at[1, b], "head")
    for b in range(2):
        r = rows(b)
        remote(psend.at[1, r, theirs], pfin.at[r], ps.at[1, b], pr.at[1, b], "head").wait_recv()
        noise = part[r, mine] + pfin[r].astype(F32)
        out[r] = updated(1, b, h, statev[h, r].astype(F32), noise)

    for copy in sent:
        copy.wait_send()


def on_device(
    latents, known, seam_mask, timesteps, block_lists, guidance,
    modulation_weight, self_weight, self_out_weight, cross_weight, cross_out_weight,
):
    mask = seam_mask.reshape(2, BLOCK)
    vmem = pl.BlockSpec(memory_space=pltpu.VMEM)
    smem = pl.BlockSpec(memory_space=pltpu.SMEM)
    hbm = pl.BlockSpec(memory_space=pl.ANY)
    dma = lambda *shape: pltpu.SemaphoreType.DMA(shape)
    return pl.pallas_call(
        kernel,
        out_shape=jax.ShapeDtypeStruct((TOK, HALF), BF16),
        in_specs=[smem, smem, vmem, vmem] + [hbm] * 7,
        out_specs=vmem,
        scratch_shapes=[
            pltpu.VMEM((2, TOK, HALF), BF16),
            pltpu.VMEM((2, TOK, HALF), BF16),
            pltpu.VMEM((2, TOK, HALF), BF16),
            pltpu.VMEM((FREQ, 4, D), BF16),
            pltpu.VMEM((3, D, HALF), BF16),
            pltpu.VMEM((HALF, D), BF16),
            pltpu.VMEM((3, D, HALF), BF16),
            pltpu.VMEM((HALF, D), BF16),
            pltpu.VMEM((STEPS, FREQ, BLOCK), F32),
            pltpu.VMEM((2, 16, BLOCK), F32),
            pltpu.VMEM((STEPS, 4, D), F32),
            pltpu.VMEM((TOK, D), BF16),
            pltpu.VMEM((TOK, D), BF16),
            pltpu.VMEM((STEPS, 5, TOK, D), BF16),
            pltpu.VMEM((2, STEPS, 8, BLOCK, HALF), BF16),
            pltpu.VMEM((STEPS, BLOCK, HALF), BF16),
            pltpu.VMEM((4, STEPS * GUIDE, D), BF16),
            pltpu.VMEM((8, TOK, BLOCK), BF16),
            pltpu.VMEM((8, TOK, BLOCK), BF16),
            pltpu.VMEM((8, HEAD_DIM + 16, TOK), F32),
            pltpu.VMEM((8, 8, TOK), F32),
            pltpu.VMEM((8, HEAD_DIM + 16, TOK), F32),
            pltpu.VMEM((8, 8, TOK), F32),
            pltpu.VMEM((TOK, HALF), BF16),
            pltpu.VMEM((TOK, HALF), BF16),
            pltpu.VMEM((TOK, D), F32),
            pltpu.VMEM((STEPS, TOK, D), BF16),
            pltpu.VMEM((TOK, D), BF16),
            pltpu.VMEM((TOK, HALF), BF16),
            dma(11), dma(2), dma(2), dma(1), dma(1),
            dma(STEPS, 4, 2), dma(STEPS, 5, 2),
            dma(3), dma(3), dma(STEPS, 3), dma(STEPS, 3),
            dma(STEPS, 8), dma(STEPS, 8), dma(STEPS, 8), dma(STEPS, 8),
            dma(STEPS, 2), dma(STEPS, 2),
        ],
        compiler_params=pltpu.CompilerParams(
            collective_id=0, has_side_effects=True, vmem_limit_bytes=56 << 20
        ),
        name="denoise",
    )(
        timesteps, block_lists, mask, guidance.reshape(STEPS * GUIDE, D),
        latents, known, modulation_weight, jnp.transpose(self_weight, (1, 0, 2)),
        self_out_weight, jnp.transpose(cross_weight, (1, 0, 2)), cross_out_weight,
    )


def solution(mesh):
    in_specs = (
        P("seq", "head"), P("seq", "head"), P("seq"), P(), P("seq", None), P(None, "seq", None),
        P(), P(None, None, "head"), P("head", None), P(None, None, "head"), P("head", None),
    )
    return jax.shard_map(
        on_device, mesh=mesh, in_specs=in_specs, out_specs=P("seq", "head"), check_vma=False
    )
```

```python
import functools
import math

import jax
import jax.numpy as jnp
from jax import lax
from jax.experimental import pallas as pl
from jax.experimental.pallas import tpu as pltpu
from jax.sharding import PartitionSpec as P

D = 1024
HALF = 512
HEAD_DIM = 64
FREQ = 256
BLOCK = 128
TOK = 256
STEPS = 2
NSEQ = 128
GUIDE = 8
MESH = pl.DeviceIdType.MESH
F32 = jnp.float32
BF16 = jnp.bfloat16
OWN, CORE, UP, DOWN, OVER = range(5)


def places(s):
    q = lax.rem(s, 4)
    wrap = lambda v: lax.rem(v + NSEQ, NSEQ)
    turn = lambda d: 16 * (s // 16) + lax.rem(lax.rem(s, 16) + 4 * d, 16)
    return dict(
        core=s + 1 - 2 * lax.rem(s, 2),
        over=4 * (s // 4) + 3 - q,
        diag=4 * (s // 4) + lax.rem(q + 2, 4),
        up=wrap(s + 4),
        down=wrap(s - 4),
        turn1=turn(1),
        turn2=turn(2),
        turn3=turn(3),
        zup=wrap(s + 16),
        zdown=wrap(s - 16),
    )


def norm(parts):
    width = sum(p.shape[1] for p in parts)
    mean = sum(jnp.sum(p, axis=1, keepdims=True) for p in parts) * (1.0 / width)
    parts = [p - mean for p in parts]
    var = sum(jnp.sum(p * p, axis=1, keepdims=True) for p in parts) * (1.0 / width)
    scale = lax.rsqrt(var + 1e-06)
    return [p * scale for p in parts]


def kernel(
    steps, lists, mask, guid, lat, known, mw, sw, sow, cw, cow,
    out,
    latv, knownv, statev, mwv, swv, sowv, cwv, cowv, acol, bias, tab, mixb, plainb, kvb, gb, gp, ab,
    qs, cqs, acc, mx, acc2, mx2, att, gud, part, psend, precv, pfin,
    lsem, hs, hr, kss, krs, kvs, kvr, gas, gar, gbs, gbr, zs, zr, cs, cr, ps, pr,
):
    s = lax.axis_index("seq")
    h = lax.axis_index("head")
    q = lax.rem(s, 4)
    c = lax.rem(s, 2)
    at = places(s)
    to = {k: {"seq": v, "head": h} for k, v in at.items()}
    to["head"] = {"seq": s, "head": 1 - h}

    loads = [
        (cw.at[1], cwv.at[1]),
        (cw.at[2], cwv.at[2]),
        (lat, latv.at[h]),
        (sw.at[1], swv.at[1]),
        (sw.at[2], swv.at[2]),
        (mw, mwv),
        (sw.at[0], swv.at[0]),
        (cw.at[0], cwv.at[0]),
        (sow, sowv),
        (cow, cowv),
        (known, knownv.at[h]),
    ]
    loads = [pltpu.make_async_copy(a, b, lsem.at[n]) for n, (a, b) in enumerate(loads)]
    for load in loads:
        load.start()

    barrier = pltpu.get_barrier_semaphore()
    for place in to.values():
        pl.semaphore_signal(barrier, inc=1, device_id=place, device_id_type=MESH)
    pl.semaphore_wait(barrier, len(to))

    def remote(src, dst, send, recv, place):
        return pltpu.make_async_remote_copy(
            src_ref=src, dst_ref=dst, send_sem=send, recv_sem=recv,
            device_id=to[place], device_id_type=MESH,
        )

    sent = []

    def send(*args):
        copy = remote(*args)
        copy.start()
        sent.append(copy)

    def rows(b):
        return pl.ds(BLOCK * b, BLOCK)

    for b in range(2):
        send(lat.at[rows(b)], latv.at[h, rows(b)], hs.at[b], hr.at[b], "head")

    loads[0].wait()
    loads[1].wait()
    guide_in = norm([guid[...].astype(F32)])[0].astype(BF16)
    for j in range(2):
        ab[q, :, HALF * j : HALF * (j + 1)] = jnp.dot(
            guide_in, cwv[j + 1], preferred_element_type=F32
        ).astype(BF16)
    for n, place in enumerate(("core", "over", "diag")):
        send(ab.at[q], ab.at[q], gas.at[n], gar.at[n], place)

    lane = lax.broadcasted_iota(jnp.int32, (1, BLOCK), 1)
    other = lax.rem(2 * s - at["core"] + NSEQ, NSEQ)
    for n, name in enumerate((s, at["core"], at["up"], at["down"], other)):
        for kb in range(2):
            shut = []
            for b in range(2):
                hit = jnp.int32(0)
                for m in range(6):
                    hit = hit | jnp.where(lists[b, m] == 2 * name + kb, 1, 0)
                shut.append(jnp.where(hit == 1, 0.0, -1e30))
            for u, base in enumerate((HEAD_DIM, 0)):
                line = jnp.where(lane == base, shut[0], jnp.where(lane == base + 1, shut[1], 0.0))
                bias[u, 2 * n + kb : 2 * n + kb + 1, :] = line

    step_row = lax.broadcasted_iota(jnp.int32, (8, BLOCK), 0)
    moment = jnp.where(
        step_row == 0, steps[0].astype(F32), jnp.where(step_row == 1, steps[1].astype(F32), steps[2].astype(F32))
    )
    which = lax.broadcasted_iota(jnp.int32, (8, BLOCK), 1).astype(F32)
    phase = moment * jnp.exp(which * (-math.log(10000.0) / (FREQ // 2)))
    for n, embed in enumerate((jnp.cos(phase), jnp.sin(phase))):
        embed = (embed / (1.0 + jnp.exp(-embed))).astype(BF16).astype(F32)
        for i in range(STEPS):
            acol[i, BLOCK * n : BLOCK * (n + 1), :] = jnp.transpose(
                jnp.broadcast_to(embed[i : i + 1, :], (BLOCK, BLOCK))
            )
    cosine = jnp.cos((moment / 1000.0 + 0.008) / 1.008 * (math.pi / 2.0))
    level = cosine * cosine
    root, rest = jnp.sqrt(level), jnp.sqrt(1.0 - level)
    coefs = []
    for i in range(STEPS):
        ratio = root[i + 1 : i + 2] / root[i : i + 1]
        line = (ratio, rest[i + 1 : i + 2] - ratio * rest[i : i + 1], root[i + 1 : i + 2], rest[i + 1 : i + 2])
        coefs.append([jnp.concatenate([x] * 4, axis=1) for x in line])

    loads[5].wait()

    def modulate(k, sums):
        row = mwv[k].astype(F32)
        scale = [jnp.concatenate([acol[i, pl.ds(k, 1), :]] * 8, axis=1) for i in range(STEPS)]
        return sums[0] + scale[0] * row, sums[1] + scale[1] * row

    zero = jnp.zeros((4, D), F32)
    tab[0], tab[1] = lax.fori_loop(0, FREQ, modulate, (zero, zero), unroll=4)

    def guide_second():
        for n, place in enumerate(("core", "over", "diag")):
            remote(ab.at[q], ab.at[q], gas.at[n], gar.at[n], place).wait_recv()
        lanes = pl.ds(pl.multiple_of(HALF * c, HALF), HALF)
        own = [ab[k, :, lanes].astype(F32) for k in range(4)]
        for i in range(STEPS):
            gp[i, 0:32, :] = jnp.concatenate(
                [o[GUIDE * i : GUIDE * (i + 1)] for o in own], axis=0
            ).astype(BF16)
            for d in range(1, 4):
                send(
                    gp.at[i, 0:32], gp.at[i, 32 * d : 32 * d + 32],
                    gbs.at[i, d - 1], gbr.at[i, d - 1], f"turn{d}",
                )

    def ring(i, src, dst):
        send(gb.at[c, i, src], gb.at[c, i, dst], zs.at[i, dst], zr.at[i, dst],
             "zup" if dst in (1, 3, 5) else "zdown")

    def across(i, slot):
        send(gb.at[c, i, slot], gb.at[c, i, slot], cs.at[i, slot], cr.at[i, slot], "core")

    def guide_third(i):
        for d in range(1, 4):
            remote(
                gp.at[i, 0:32], gp.at[i, 32 * d : 32 * d + 32],
                gbs.at[i, d - 1], gbr.at[i, d - 1], f"turn{d}",
            ).wait_recv()
        for p in range(4):
            cols = slice(BLOCK * p, BLOCK * (p + 1))
            y = gp[i, :, cols].astype(F32)
            gb[c, i, 0, :, cols] = jnp.where(c == 1, jnp.transpose(y), y).astype(BF16)
        ring(i, 0, 1)
        ring(i, 0, 2)
        across(i, 0)

    onward = {1: 3, 2: 4, 3: 5, 4: 6, 6: 7}

    def hop(i, *slots):
        for slot in slots:
            remote(gb.at[c, i, 0], gb.at[c, i, slot], zs.at[i, slot], zr.at[i, slot],
                   "zup").wait_recv()
            if slot in onward:
                ring(i, slot, onward[slot])
            across(i, slot)

    lane = lax.broadcasted_iota(jnp.int32, (1, BLOCK), 1)
    low = jnp.where(lane < HEAD_DIM, 1.0, 0.0).astype(BF16)
    low_f = lax.broadcasted_iota(jnp.int32, (TOK, BLOCK), 1) < HEAD_DIM
    keep = (low, (1.0 - low.astype(F32)).astype(BF16))

    def normalize(b, state):
        r = rows(b)
        normed = norm([state[0, r].astype(F32), state[1, r].astype(F32)])
        return r, normed

    def mix(i, b, state):
        r, normed = normalize(b, state)
        for n in range(2):
            cols = slice(HALF * n, HALF * (n + 1))
            mixb[r, cols] = (normed[n] * (1.0 + tab[i, 1:2, cols]) + tab[i, 0:1, cols]).astype(BF16)
            plainb[r, cols] = normed[n].astype(BF16)

    def keys_values(i, b):
        r = rows(b)
        x = mixb[r, :]
        for j in range(2):

            def tile(t, _):
                w = swv[1 + j, :, pl.ds(pl.multiple_of(256 * t, 256), 256)]
                y = jnp.dot(x, w, preferred_element_type=F32)
                if j == 1:
                    y = jnp.concatenate(
                        [jnp.transpose(y[:, BLOCK * u : BLOCK * (u + 1)]) for u in range(2)], axis=1
                    )
                cols = pl.ds(pl.multiple_of(HALF * j + 256 * t, 256), 256)
                kvb[i, OWN, r, cols] = y.astype(BF16)
                return 0

            lax.fori_loop(0, 2, tile, 0, unroll=True)
        for n, (slot, place) in enumerate(((CORE, "core"), (DOWN, "up"), (UP, "down"))):
            send(kvb.at[i, OWN, r], kvb.at[i, slot, r], kvs.at[i, n, b], kvr.at[i, slot, b], place)

        @pl.when(q * (3 - q) > 0)
        def _():
            remote(kvb.at[i, OWN, r], kvb.at[i, OVER, r], kvs.at[i, 3, b], kvr.at[i, OVER, b], "over").start()

        sent.append(remote(kvb.at[i, OWN, r], kvb.at[i, OVER, r], kvs.at[i, 3, b], kvr.at[i, OVER, b], "over"))

    def arrived(i, slot, b):
        remote(kvb.at[i, OWN, rows(b)], kvb.at[i, slot, rows(b)], kvs.at[i, 0, b],
               kvr.at[i, slot, b], "core").wait_recv()

    def relay(i, b):
        arrived(i, UP, b)
        arrived(i, DOWN, b)
        r = rows(b)

        @pl.when(q * (3 - q) == 0)
        def _():
            remote(kvb.at[i, UP + q // 3, r], kvb.at[i, OVER, r], kvs.at[i, 3, b], kvr.at[i, OVER, b], "over").start()

    row_id = lax.broadcasted_iota(jnp.int32, (TOK, BLOCK), 0) // BLOCK
    lane_id = lax.broadcasted_iota(jnp.int32, (TOK, BLOCK), 1)

    def queries(x_ref, w_ref, dst, marked):
        def tile(t, _):
            w = w_ref[0, :, pl.ds(pl.multiple_of(256 * t, 256), 256)]
            y = jnp.dot(x_ref[...], w, preferred_element_type=F32)
            y = y.astype(BF16).astype(F32) * (1.0 / math.sqrt(HEAD_DIM))
            for u in range(2):
                z = y[:, BLOCK * u : BLOCK * (u + 1)]
                mark_a = jnp.where(lane_id == HEAD_DIM + row_id, 1.0, 0.0) if marked else 0.0
                mark_b = jnp.where(lane_id == row_id, 1.0, 0.0) if marked else 0.0
                dst[4 * t + 2 * u] = jnp.where(low_f, z, mark_a).astype(BF16)
                dst[4 * t + 2 * u + 1] = jnp.where(low_f, mark_b, z).astype(BF16)
            return 0

        lax.fori_loop(0, 2, tile, 0, unroll=True)

    ones = jnp.ones((16, TOK), BF16)

    def attend(q_ref, tiles, first, sums, peaks):
        def pair(p, _):
            lanes = pl.ds(pl.multiple_of(BLOCK * p, BLOCK), BLOCK)
            loaded = [load(lanes) for load, _ in tiles]
            for u in range(2):
                head = 2 * p + u
                scores = []
                for (k, _), (_, marks) in zip(loaded, tiles):
                    k = k if marks is None else k * keep[u] + marks[u]
                    scores.append(
                        lax.dot_general(
                            k, q_ref[head], (((1,), (1,)), ((), ())), preferred_element_type=F32
                        )
                    )
                peak = functools.reduce(
                    jnp.maximum, [jnp.max(x, axis=0, keepdims=True) for x in scores]
                )
                if not first:
                    old = peaks[head, 0:1, :]
                    peak = jnp.maximum(peak, old)
                mixed = None
                for x, (_, v) in zip(scores, loaded):
                    v = jnp.concatenate([v[HEAD_DIM * u : HEAD_DIM * (u + 1)], ones], axis=0)
                    y = jnp.dot(v, jnp.exp(x - peak).astype(BF16), preferred_element_type=F32)
                    mixed = y if mixed is None else mixed + y
                if not first:
                    mixed = mixed + sums[head] * jnp.exp(old - peak)
                sums[head] = mixed
                peaks[head, 0:1, :] = peak
            return 0

        lax.fori_loop(0, 4, pair, 0, unroll=True)

    def attend_tiles(i, *slots):
        def tile(slot):
            marks = [
                jnp.concatenate(
                    [
                        jnp.broadcast_to(
                            bias[u, 2 * slot + b : 2 * slot + b + 1, :], (BLOCK, BLOCK)
                        )
                        for b in range(2)
                    ],
                    axis=0,
                ).astype(BF16)
                for u in range(2)
            ]

            def load(lanes):
                high_lanes = pl.ds(HALF + lanes.start, BLOCK)
                v = [kvb[i, slot, BLOCK * b : BLOCK * (b + 1), high_lanes] for b in range(2)]
                return kvb[i, slot, :, lanes], jnp.concatenate(v, axis=1)

            return load, marks

        attend(qs, [tile(slot) for slot in slots], slots[0] == OWN, acc, mx)

    def attend_guide(i, *chunks):
        def tile(n):
            def load(lanes):
                k = gb[0, i, 2 * n : 2 * n + 2, :, lanes].reshape(TOK, BLOCK)
                v = [gb[1, i, 2 * n + b, :, lanes] for b in range(2)]
                return k, jnp.concatenate(v, axis=1)

            return load, None

        attend(cqs, [tile(n) for n in chunks], chunks[0] == 0, acc2, mx2)

    def crossed(i, *slots):
        for slot in slots:
            remote(gb.at[c, i, 0], gb.at[1 - c, i, slot], cs.at[i, slot], cr.at[i, slot],
                   "core").wait_recv()

    def finish(dst, sums):
        def pair(p, _):
            y = [
                sums[2 * p + u, 0:HEAD_DIM, :] / sums[2 * p + u, HEAD_DIM : HEAD_DIM + 1, :]
                for u in range(2)
            ]
            y = jnp.concatenate(y, axis=0)
            for b in range(2):
                dst[rows(b), pl.ds(pl.multiple_of(BLOCK * p, BLOCK), BLOCK)] = jnp.transpose(
                    y[:, BLOCK * b : BLOCK * (b + 1)]
                ).astype(BF16)
            return 0

        lax.fori_loop(0, 4, pair, 0, unroll=True)

    def project(i, b, x_ref, w_ref, gate, first):
        r = rows(b)
        x = x_ref[r, :]

        def tile(t, _):
            cols = pl.ds(pl.multiple_of(256 * t, 256), 256)
            y = jnp.dot(x, w_ref[:, cols], preferred_element_type=F32) * tab[i, gate : gate + 1, cols]
            y = y if first else y + part[r, cols]
            part[r, cols] = y
            if not first:
                psend[i, r, cols] = y.astype(BF16)
            return 0

        lax.fori_loop(0, 4, tile, 0, unroll=True)

    def seam(b):
        flags = jnp.broadcast_to(mask[b : b + 1, :].astype(F32), (BLOCK, BLOCK))
        wide = jnp.transpose(flags)
        return jnp.concatenate([wide] * 4, axis=1) > 0.5

    def updated(i, b, n, state, noise):
        r = rows(b)
        moved = coefs[i][0] * state + coefs[i][1] * noise
        kept = coefs[i][2] * knownv[n, r].astype(F32) + coefs[i][3] * latv[n, r].astype(F32)
        return jnp.where(seam(b), moved, kept).astype(BF16)

    loads[2].wait()
    loads[3].wait()
    loads[4].wait()
    for b in range(2):
        remote(lat.at[rows(b)], latv.at[1 - h, rows(b)], hs.at[b], hr.at[b], "head").wait_recv()
        mix(0, b, latv)
        keys_values(0, b)
        if b == 0:
            guide_second()
    loads[6].wait()
    loads[7].wait()
    send(known, knownv.at[h], kss.at[0], krs.at[0], "head")
    queries(mixb, swv, qs, True)
    guide_third(0)
    attend_tiles(0, OWN)
    hop(0, 1, 2)
    relay(0, 0)
    queries(plainb, cwv, cqs, False)
    arrived(0, CORE, 0)
    arrived(0, CORE, 1)
    attend_tiles(0, CORE)
    hop(0, 3, 4)
    relay(0, 1)
    attend_tiles(0, UP, DOWN)
    hop(0, 5, 6)
    crossed(0, 0, 1)
    attend_guide(0, 0)
    hop(0, 7)
    guide_third(1)
    arrived(0, OVER, 0)
    arrived(0, OVER, 1)
    attend_tiles(0, OVER)
    finish(att, acc)
    loads[8].wait()
    loads[9].wait()
    for b in range(2):
        project(0, b, att, sowv, 2, True)
    crossed(0, 2, 3)
    attend_guide(0, 1)
    hop(1, 1, 2)
    crossed(0, 4, 5, 6, 7)
    attend_guide(0, 2, 3)
    finish(gud, acc2)
    for b in range(2):
        project(0, b, gud, cowv, 3, False)
        send(psend.at[0, rows(b)], precv.at[rows(b)], ps.at[0, b], pr.at[0, b], "head")
    hop(1, 3, 4)

    loads[10].wait()
    remote(known, knownv.at[1 - h], kss.at[0], krs.at[0], "head").wait_recv()
    for b in range(2):
        r = rows(b)
        remote(psend.at[0, r], precv.at[r], ps.at[0, b], pr.at[0, b], "head").wait_recv()
        for n in range(2):
            cols = slice(HALF * n, HALF * (n + 1))
            noise = part[r, cols] + precv[r, cols].astype(F32)
            statev[n, r] = updated(0, b, n, latv[n, r].astype(F32), noise)
        mix(1, b, statev)
        keys_values(1, b)
        if b == 0:
            hop(1, 5, 6)
    hop(1, 7)
    queries(mixb, swv, qs, True)
    attend_tiles(1, OWN)
    queries(plainb, cwv, cqs, False)
    relay(1, 0)
    crossed(1, *range(8))
    attend_guide(1, 0, 1)
    relay(1, 1)
    attend_guide(1, 2, 3)
    arrived(1, CORE, 0)
    arrived(1, CORE, 1)
    attend_tiles(1, CORE)
    finish(gud, acc2)
    for b in range(2):
        project(1, b, gud, cowv, 3, True)
    attend_tiles(1, UP, DOWN)
    arrived(1, OVER, 0)
    arrived(1, OVER, 1)
    attend_tiles(1, OVER)
    finish(att, acc)
    mine = pl.ds(pl.multiple_of(HALF * h, HALF), HALF)
    theirs = pl.ds(pl.multiple_of(HALF * (1 - h), HALF), HALF)
    for b in range(2):
        project(1, b, att, sowv, 2, False)
        send(psend.at[1, rows(b), theirs], pfin.at[rows(b)], ps.at[1, b], pr.at[1, b], "head")
    for b in range(2):
        r = rows(b)
        remote(psend.at[1, r, theirs], pfin.at[r], ps.at[1, b], pr.at[1, b], "head").wait_recv()
        noise = part[r, mine] + pfin[r].astype(F32)
        out[r] = updated(1, b, h, statev[h, r].astype(F32), noise)

    for copy in sent:
        copy.wait_send()


def on_device(
    latents, known, seam_mask, timesteps, block_lists, guidance,
    modulation_weight, self_weight, self_out_weight, cross_weight, cross_out_weight,
):
    mask = seam_mask.reshape(2, BLOCK)
    vmem = pl.BlockSpec(memory_space=pltpu.VMEM)
    smem = pl.BlockSpec(memory_space=pltpu.SMEM)
    hbm = pl.BlockSpec(memory_space=pl.ANY)
    dma = lambda *shape: pltpu.SemaphoreType.DMA(shape)
    return pl.pallas_call(
        kernel,
        out_shape=jax.ShapeDtypeStruct((TOK, HALF), BF16),
        in_specs=[smem, smem, vmem, vmem] + [hbm] * 7,
        out_specs=vmem,
        scratch_shapes=[
            pltpu.VMEM((2, TOK, HALF), BF16),
            pltpu.VMEM((2, TOK, HALF), BF16),
            pltpu.VMEM((2, TOK, HALF), BF16),
            pltpu.VMEM((FREQ, 4, D), BF16),
            pltpu.VMEM((3, D, HALF), BF16),
            pltpu.VMEM((HALF, D), BF16),
            pltpu.VMEM((3, D, HALF), BF16),
            pltpu.VMEM((HALF, D), BF16),
            pltpu.VMEM((STEPS, FREQ, BLOCK), F32),
            pltpu.VMEM((2, 16, BLOCK), F32),
            pltpu.VMEM((STEPS, 4, D), F32),
            pltpu.VMEM((TOK, D), BF16),
            pltpu.VMEM((TOK, D), BF16),
            pltpu.VMEM((STEPS, 5, TOK, D), BF16),
            pltpu.VMEM((2, STEPS, 8, BLOCK, HALF), BF16),
            pltpu.VMEM((STEPS, BLOCK, HALF), BF16),
            pltpu.VMEM((4, STEPS * GUIDE, D), BF16),
            pltpu.VMEM((8, TOK, BLOCK), BF16),
            pltpu.VMEM((8, TOK, BLOCK), BF16),
            pltpu.VMEM((8, HEAD_DIM + 16, TOK), F32),
            pltpu.VMEM((8, 8, TOK), F32),
            pltpu.VMEM((8, HEAD_DIM + 16, TOK), F32),
            pltpu.VMEM((8, 8, TOK), F32),
            pltpu.VMEM((TOK, HALF), BF16),
            pltpu.VMEM((TOK, HALF), BF16),
            pltpu.VMEM((TOK, D), F32),
            pltpu.VMEM((STEPS, TOK, D), BF16),
            pltpu.VMEM((TOK, D), BF16),
            pltpu.VMEM((TOK, HALF), BF16),
            dma(11), dma(2), dma(2), dma(1), dma(1),
            dma(STEPS, 4, 2), dma(STEPS, 5, 2),
            dma(3), dma(3), dma(STEPS, 3), dma(STEPS, 3),
            dma(STEPS, 8), dma(STEPS, 8), dma(STEPS, 8), dma(STEPS, 8),
            dma(STEPS, 2), dma(STEPS, 2),
        ],
        compiler_params=pltpu.CompilerParams(
            collective_id=0, has_side_effects=True, vmem_limit_bytes=56 << 20
        ),
        name="denoise",
    )(
        timesteps, block_lists, mask, guidance.reshape(STEPS * GUIDE, D),
        latents, known, modulation_weight, jnp.transpose(self_weight, (1, 0, 2)),
        self_out_weight, jnp.transpose(cross_weight, (1, 0, 2)), cross_out_weight,
    )


def solution(mesh):
    in_specs = (
        P("seq", "head"), P("seq", "head"), P("seq"), P(), P("seq", None), P(None, "seq", None),
        P(), P(None, None, "head"), P("head", None), P(None, None, "head"), P("head", None),
    )
    return jax.shard_map(
        on_device, mesh=mesh, in_specs=in_specs, out_specs=P("seq", "head"), check_vma=False
    )
```

```python
import functools
import math

import jax
import jax.numpy as jnp
from jax import lax
from jax.experimental import pallas as pl
from jax.experimental.pallas import tpu as pltpu
from jax.sharding import PartitionSpec as P

D = 1024
HALF = 512
HEAD_DIM = 64
FREQ = 256
BLOCK = 128
MAXK = 6
TOK = 256
STEPS = 2
NSEQ = 128
GUIDE = 8
MESH = pl.DeviceIdType.MESH
F32 = jnp.float32
BF16 = jnp.bfloat16
OWN, CORE, UP, DOWN, OVER = range(5)


def places(s):
    q = lax.rem(s, 4)
    wrap = lambda v: lax.rem(v + NSEQ, NSEQ)
    turn = lambda d: 16 * (s // 16) + lax.rem(lax.rem(s, 16) + 4 * d, 16)
    return dict(
        core=s + 1 - 2 * lax.rem(s, 2),
        over=4 * (s // 4) + 3 - q,
        diag=4 * (s // 4) + lax.rem(q + 2, 4),
        up=wrap(s + 4),
        down=wrap(s - 4),
        turn1=turn(1),
        turn2=turn(2),
        turn3=turn(3),
        zup=wrap(s + 16),
        zdown=wrap(s - 16),
    )


def norm(parts):
    width = sum(p.shape[1] for p in parts)
    mean = sum(jnp.sum(p, axis=1, keepdims=True) for p in parts) * (1.0 / width)
    parts = [p - mean for p in parts]
    var = sum(jnp.sum(p * p, axis=1, keepdims=True) for p in parts) * (1.0 / width)
    scale = lax.rsqrt(var + 1e-06)
    return [p * scale for p in parts]


def kernel(
    steps, lists, mask, guid, lat, known, mw, sw, sow, cw, cow,
    out,
    latv, knownv, statev, mwv, swv, sowv, cwv, cowv, acol, bias, tile_bias, seam, tab, mixb, plainb, kv0, kv1, gb, gp, ab,
    qs, cqs, acc, mx, acc2, mx2, att, gud, part, psend, precv, pfin,
    lsem, hs, hr, kss, krs, kvs, kvr, gas, gar, gbs, gbr, zs, zr, cs, cr, ps, pr,
):
    s = lax.axis_index("seq")
    h = lax.axis_index("head")
    q = lax.rem(s, 4)
    c = lax.rem(s, 2)
    kv = (kv0, kv1)
    at = places(s)
    to = {k: {"seq": v, "head": h} for k, v in at.items()}
    to["head"] = {"seq": s, "head": 1 - h}

    loads = [
        (cw.at[1], cwv.at[1]),
        (cw.at[2], cwv.at[2]),
        (lat, latv.at[h]),
        (sw.at[1], swv.at[1]),
        (sw.at[2], swv.at[2]),
        (mw, mwv),
        (sw.at[0], swv.at[0]),
        (cw.at[0], cwv.at[0]),
        (sow, sowv),
        (cow, cowv),
        (known, knownv.at[h]),
    ]
    loads = [pltpu.make_async_copy(a, b, lsem.at[n]) for n, (a, b) in enumerate(loads)]
    for load in loads:
        load.start()

    barrier = pltpu.get_barrier_semaphore()
    for place in to.values():
        pl.semaphore_signal(barrier, inc=1, device_id=place, device_id_type=MESH)
    pl.semaphore_wait(barrier, len(to))

    def remote(src, dst, send, recv, place):
        return pltpu.make_async_remote_copy(
            src_ref=src, dst_ref=dst, send_sem=send, recv_sem=recv,
            device_id=to[place], device_id_type=MESH,
        )

    sent = []

    def send(*args):
        copy = remote(*args)
        copy.start()
        sent.append(copy)

    def rows(b):
        return pl.ds(BLOCK * b, BLOCK)

    for b in range(2):
        send(lat.at[rows(b)], latv.at[h, rows(b)], hs.at[b], hr.at[b], "head")

    loads[0].wait()
    loads[1].wait()
    guide_in = norm([guid[...].astype(F32)])[0].astype(BF16)
    for j in range(2):
        ab[q, :, HALF * j : HALF * (j + 1)] = jnp.dot(
            guide_in, cwv[j + 1], preferred_element_type=F32
        ).astype(BF16)
    for n, place in enumerate(("core", "over", "diag")):
        send(ab.at[q], ab.at[q], gas.at[n], gar.at[n], place)

    lane = lax.broadcasted_iota(jnp.int32, (1, BLOCK), 1)
    other = lax.rem(2 * s - at["core"] + NSEQ, NSEQ)
    names = (s, at["core"], at["up"], at["down"], other)
    picks = []
    for b in range(2):
        picks.append([])
        for m in range(MAXK):
            entry = lists[b, m]
            spot = jnp.int32(0)
            for n, name in enumerate(names):
                for kb in range(2):
                    spot = jnp.where(entry == 2 * name + kb, 2 * n + kb, spot)
            picks[b].append(spot)
            shut = jnp.where(entry >= 0, 0.0, -1e30)
            for u, base in enumerate((HEAD_DIM, 0)):
                bias[u, MAXK * b + m : MAXK * b + m + 1, :] = jnp.where(lane == base + b, shut, 0.0)

    for b in range(2):
        flags = mask[pl.ds(BLOCK * b, BLOCK)].astype(F32)
        seam[pl.ds(BLOCK * b, BLOCK), :] = jnp.transpose(
            jnp.broadcast_to(flags[None, :], (BLOCK, BLOCK))
        )

    for n, name in enumerate(names):
        for kb in range(2):
            shut = []
            for b in range(2):
                hit = jnp.int32(0)
                for m in range(MAXK):
                    hit = hit | jnp.where(lists[b, m] == 2 * name + kb, 1, 0)
                shut.append(jnp.where(hit == 1, 0.0, -1e30))
            for u, base in enumerate((HEAD_DIM, 0)):
                line = jnp.where(lane == base, shut[0], jnp.where(lane == base + 1, shut[1], 0.0))
                tile_bias[u, 2 * n + kb : 2 * n + kb + 1, :] = line

    step_row = lax.broadcasted_iota(jnp.int32, (8, BLOCK), 0)
    moment = jnp.where(
        step_row == 0, steps[0].astype(F32), jnp.where(step_row == 1, steps[1].astype(F32), steps[2].astype(F32))
    )
    which = lax.broadcasted_iota(jnp.int32, (8, BLOCK), 1).astype(F32)
    phase = moment * jnp.exp(which * (-math.log(10000.0) / (FREQ // 2)))
    for n, embed in enumerate((jnp.cos(phase), jnp.sin(phase))):
        embed = (embed / (1.0 + jnp.exp(-embed))).astype(BF16).astype(F32)
        for i in range(STEPS):
            acol[i, BLOCK * n : BLOCK * (n + 1), :] = jnp.transpose(
                jnp.broadcast_to(embed[i : i + 1, :], (BLOCK, BLOCK))
            )
    cosine = jnp.cos((moment / 1000.0 + 0.008) / 1.008 * (math.pi / 2.0))
    level = cosine * cosine
    root, rest = jnp.sqrt(level), jnp.sqrt(1.0 - level)
    coefs = []
    for i in range(STEPS):
        ratio = root[i + 1 : i + 2] / root[i : i + 1]
        line = (ratio, rest[i + 1 : i + 2] - ratio * rest[i : i + 1], root[i + 1 : i + 2], rest[i + 1 : i + 2])
        coefs.append([jnp.concatenate([x] * 4, axis=1) for x in line])

    loads[5].wait()

    def modulate(k, sums):
        row = mwv[k].astype(F32)
        scale = [jnp.concatenate([acol[i, pl.ds(k, 1), :]] * 8, axis=1) for i in range(STEPS)]
        return sums[0] + scale[0] * row, sums[1] + scale[1] * row

    zero = jnp.zeros((4, D), F32)
    tab[0], tab[1] = lax.fori_loop(0, FREQ, modulate, (zero, zero), unroll=4)

    def guide_second():
        for n, place in enumerate(("core", "over", "diag")):
            remote(ab.at[q], ab.at[q], gas.at[n], gar.at[n], place).wait_recv()
        lanes = pl.ds(pl.multiple_of(HALF * c, HALF), HALF)
        own = [ab[k, :, lanes].astype(F32) for k in range(4)]
        for i in range(STEPS):
            gp[i, 0:32, :] = jnp.concatenate(
                [o[GUIDE * i : GUIDE * (i + 1)] for o in own], axis=0
            ).astype(BF16)
            for d in range(1, 4):
                send(
                    gp.at[i, 0:32], gp.at[i, 32 * d : 32 * d + 32],
                    gbs.at[i, d - 1], gbr.at[i, d - 1], f"turn{d}",
                )

    def ring(i, src, dst):
        send(gb.at[c, i, src], gb.at[c, i, dst], zs.at[i, dst], zr.at[i, dst],
             "zup" if dst in (1, 3, 5) else "zdown")

    def across(i, slot):
        send(gb.at[c, i, slot], gb.at[c, i, slot], cs.at[i, slot], cr.at[i, slot], "core")

    def guide_third(i):
        for d in range(1, 4):
            remote(
                gp.at[i, 0:32], gp.at[i, 32 * d : 32 * d + 32],
                gbs.at[i, d - 1], gbr.at[i, d - 1], f"turn{d}",
            ).wait_recv()
        for p in range(4):
            cols = slice(BLOCK * p, BLOCK * (p + 1))
            y = gp[i, :, cols].astype(F32)
            gb[c, i, 0, :, cols] = jnp.where(c == 1, jnp.transpose(y), y).astype(BF16)
        ring(i, 0, 1)
        ring(i, 0, 2)
        across(i, 0)

    onward = {1: 3, 2: 4, 3: 5, 4: 6, 6: 7}

    def hop(i, *slots):
        for slot in slots:
            remote(gb.at[c, i, 0], gb.at[c, i, slot], zs.at[i, slot], zr.at[i, slot],
                   "zup").wait_recv()
            if slot in onward:
                ring(i, slot, onward[slot])
            across(i, slot)

    lane = lax.broadcasted_iota(jnp.int32, (1, BLOCK), 1)
    low = jnp.where(lane < HEAD_DIM, 1.0, 0.0).astype(BF16)
    low_f = lax.broadcasted_iota(jnp.int32, (TOK, BLOCK), 1) < HEAD_DIM
    keep = (low, (1.0 - low.astype(F32)).astype(BF16))

    def normalize(b, state):
        r = rows(b)
        normed = norm([state[0, r].astype(F32), state[1, r].astype(F32)])
        return r, normed

    def mix(i, b, state):
        r, normed = normalize(b, state)
        for n in range(2):
            cols = slice(HALF * n, HALF * (n + 1))
            mixb[r, cols] = (normed[n] * (1.0 + tab[i, 1:2, cols]) + tab[i, 0:1, cols]).astype(BF16)
            plainb[r, cols] = normed[n].astype(BF16)

    def chunk(i, n, j):
        return kv[i].at[n, :, pl.ds(HALF * j, HALF)]

    def over(i, b, j, n):
        return remote(
            chunk(i, n, j), chunk(i, 2 * OVER + b, j), kvs.at[i, 3, b, j], kvr.at[i, OVER, b, j], "over"
        )

    def keys_values(i, b):
        x = mixb[rows(b), :]
        for j in range(2):

            def tile(t, _):
                w = swv[1 + j, :, pl.ds(pl.multiple_of(256 * t, 256), 256)]
                y = jnp.dot(x, w, preferred_element_type=F32)
                if j == 1:
                    y = jnp.concatenate(
                        [jnp.transpose(y[:, BLOCK * u : BLOCK * (u + 1)]) for u in range(2)], axis=1
                    )
                cols = pl.ds(pl.multiple_of(HALF * j + 256 * t, 256), 256)
                kv[i][b, :, cols] = y.astype(BF16)
                return 0

            lax.fori_loop(0, 2, tile, 0, unroll=True)
            for n, (slot, place) in enumerate(((DOWN, "up"), (UP, "down"), (CORE, "core"))):
                send(
                    chunk(i, b, j), chunk(i, 2 * slot + b, j),
                    kvs.at[i, n, b, j], kvr.at[i, slot, b, j], place,
                )

            @pl.when(q * (3 - q) > 0)
            def _():
                over(i, b, j, b).start()

            sent.append(over(i, b, j, b))

    def arrived(i, slot, b):
        for j in range(2):
            arrived_part(i, slot, b, j)

    def arrived_part(i, slot, b, j):
        remote(
            chunk(i, b, j), chunk(i, 2 * slot + b, j), kvs.at[i, 0, b, j], kvr.at[i, slot, b, j], "core"
        ).wait_recv()

    def relay(i, b):
        for j in range(2):
            arrived_part(i, UP, b, j)
            arrived_part(i, DOWN, b, j)

            @pl.when(q * (3 - q) == 0)
            def _():
                over(i, b, j, 2 * (UP + q // 3) + b).start()

    row_id = lax.broadcasted_iota(jnp.int32, (TOK, BLOCK), 0) // BLOCK
    lane_id = lax.broadcasted_iota(jnp.int32, (TOK, BLOCK), 1)

    def queries(x_ref, w_ref, dst, marked):
        def tile(t, _):
            w = w_ref[0, :, pl.ds(pl.multiple_of(256 * t, 256), 256)]
            y = jnp.dot(x_ref[...], w, preferred_element_type=F32)
            y = y.astype(BF16).astype(F32) * (1.0 / math.sqrt(HEAD_DIM))
            for u in range(2):
                z = y[:, BLOCK * u : BLOCK * (u + 1)]
                mark_a = jnp.where(lane_id == HEAD_DIM + row_id, 1.0, 0.0) if marked else 0.0
                mark_b = jnp.where(lane_id == row_id, 1.0, 0.0) if marked else 0.0
                dst[4 * t + 2 * u] = jnp.where(low_f, z, mark_a).astype(BF16)
                dst[4 * t + 2 * u + 1] = jnp.where(low_f, mark_b, z).astype(BF16)
            return 0

        lax.fori_loop(0, 2, tile, 0, unroll=True)

    ones = jnp.ones((16, TOK), BF16)

    def attend(q_ref, tiles, first, sums, peaks):
        def pair(p, _):
            lanes = pl.ds(pl.multiple_of(BLOCK * p, BLOCK), BLOCK)
            loaded = [load(lanes) for load, _ in tiles]
            for u in range(2):
                head = 2 * p + u
                scores = []
                for (k, _), (_, marks) in zip(loaded, tiles):
                    k = k if marks is None else k * keep[u] + marks[u]
                    scores.append(
                        lax.dot_general(
                            k, q_ref[head], (((1,), (1,)), ((), ())), preferred_element_type=F32
                        )
                    )
                peak = functools.reduce(
                    jnp.maximum, [jnp.max(x, axis=0, keepdims=True) for x in scores]
                )
                if not first:
                    old = peaks[head, 0:1, :]
                    peak = jnp.maximum(peak, old)
                mixed = None
                for x, (_, v) in zip(scores, loaded):
                    v = jnp.concatenate([v[HEAD_DIM * u : HEAD_DIM * (u + 1)], ones], axis=0)
                    y = jnp.dot(v, jnp.exp(x - peak).astype(BF16), preferred_element_type=F32)
                    mixed = y if mixed is None else mixed + y
                if not first:
                    mixed = mixed + sums[head] * jnp.exp(old - peak)
                sums[head] = mixed
                peaks[head, 0:1, :] = peak
            return 0

        lax.fori_loop(0, 4, pair, 0, unroll=True)

    def attend_tiles(i, *slots):
        def tile(slot):
            marks = [
                jnp.concatenate(
                    [jnp.broadcast_to(tile_bias[u, n : n + 1, :], (BLOCK, BLOCK)) for n in (2 * slot, 2 * slot + 1)],
                    axis=0,
                ).astype(BF16)
                for u in range(2)
            ]

            def load(lanes):
                high_lanes = pl.ds(HALF + lanes.start, BLOCK)
                v = [kv[i][2 * slot + b, :, high_lanes] for b in range(2)]
                k = kv[i][2 * slot : 2 * slot + 2, :, lanes].reshape(TOK, BLOCK)
                return k, jnp.concatenate(v, axis=1)

            return load, marks

        attend(qs, [tile(slot) for slot in slots], slots[0] == OWN, acc, mx)

    wide_ones = jnp.ones((16, MAXK * BLOCK), BF16)

    def attend_listed(i, b):
        marks = [
            jnp.concatenate(
                [
                    jnp.broadcast_to(bias[u, n : n + 1, :], (BLOCK, BLOCK))
                    for n in range(MAXK * b, MAXK * b + MAXK)
                ],
                axis=0,
            ).astype(BF16)
            for u in range(2)
        ]

        def pair(p, _):
            lanes = pl.ds(pl.multiple_of(BLOCK * p, BLOCK), BLOCK)
            high_lanes = pl.ds(pl.multiple_of(HALF + BLOCK * p, BLOCK), BLOCK)
            k = jnp.concatenate([kv[i][spot, :, lanes] for spot in picks[b]], axis=0)
            v = jnp.concatenate([kv[i][spot, :, high_lanes] for spot in picks[b]], axis=1)
            mixed = []
            for u in range(2):
                scores = lax.dot_general(
                    k * keep[u] + marks[u], qs[2 * p + u, rows(b), :],
                    (((1,), (1,)), ((), ())), preferred_element_type=F32,
                )
                weights = jnp.exp(scores - jnp.max(scores, axis=0, keepdims=True)).astype(BF16)
                vu = jnp.concatenate([v[HEAD_DIM * u : HEAD_DIM * (u + 1)], wide_ones], axis=0)
                y = jnp.dot(vu, weights, preferred_element_type=F32)
                mixed.append(y[0:HEAD_DIM] / y[HEAD_DIM : HEAD_DIM + 1])
            att[rows(b), lanes] = jnp.transpose(jnp.concatenate(mixed, axis=0)).astype(BF16)
            return 0

        lax.fori_loop(0, 4, pair, 0, unroll=True)

    def attend_guide(i, *chunks):
        def tile(n):
            def load(lanes):
                k = gb[0, i, 2 * n : 2 * n + 2, :, lanes].reshape(TOK, BLOCK)
                v = [gb[1, i, 2 * n + b, :, lanes] for b in range(2)]
                return k, jnp.concatenate(v, axis=1)

            return load, None

        attend(cqs, [tile(n) for n in chunks], chunks[0] == 0, acc2, mx2)

    def crossed(i, *slots):
        for slot in slots:
            remote(gb.at[c, i, 0], gb.at[1 - c, i, slot], cs.at[i, slot], cr.at[i, slot],
                   "core").wait_recv()

    def finish(dst, sums):
        def pair(p, _):
            y = [
                sums[2 * p + u, 0:HEAD_DIM, :] / sums[2 * p + u, HEAD_DIM : HEAD_DIM + 1, :]
                for u in range(2)
            ]
            y = jnp.concatenate(y, axis=0)
            for b in range(2):
                dst[rows(b), pl.ds(pl.multiple_of(BLOCK * p, BLOCK), BLOCK)] = jnp.transpose(
                    y[:, BLOCK * b : BLOCK * (b + 1)]
                ).astype(BF16)
            return 0

        lax.fori_loop(0, 4, pair, 0, unroll=True)

    def project(i, b, x_ref, w_ref, gate, first):
        r = rows(b)
        x = x_ref[r, :]

        def tile(t, _):
            cols = pl.ds(pl.multiple_of(256 * t, 256), 256)
            y = jnp.dot(x, w_ref[:, cols], preferred_element_type=F32) * tab[i, gate : gate + 1, cols]
            y = y if first else y + part[r, cols]
            part[r, cols] = y
            if not first:
                psend[i, r, cols] = y.astype(BF16)
            return 0

        lax.fori_loop(0, 4, tile, 0, unroll=True)

    def updated(i, b, n, state, noise):
        r = rows(b)
        moved = coefs[i][0] * state + coefs[i][1] * noise
        kept = coefs[i][2] * knownv[n, r].astype(F32) + coefs[i][3] * latv[n, r].astype(F32)
        flags = jnp.concatenate([seam[r, :]] * 4, axis=1) > 0.5
        return jnp.where(flags, moved, kept).astype(BF16)

    loads[2].wait()
    loads[3].wait()
    loads[4].wait()
    for b in range(2):
        remote(lat.at[rows(b)], latv.at[1 - h, rows(b)], hs.at[b], hr.at[b], "head").wait_recv()
        mix(0, b, latv)
        keys_values(0, b)
        if b == 0:
            guide_second()
    loads[6].wait()
    loads[7].wait()
    send(known, knownv.at[h], kss.at[0], krs.at[0], "head")
    queries(mixb, swv, qs, True)
    guide_third(0)
    attend_tiles(0, OWN)
    hop(0, 1, 2)
    relay(0, 0)
    queries(plainb, cwv, cqs, False)
    arrived(0, CORE, 0)
    arrived(0, CORE, 1)
    attend_tiles(0, CORE)
    hop(0, 3, 4)
    relay(0, 1)
    attend_tiles(0, UP, DOWN)
    hop(0, 5, 6)
    crossed(0, 0, 1)
    attend_guide(0, 0)
    hop(0, 7)
    guide_third(1)
    arrived(0, OVER, 0)
    arrived(0, OVER, 1)
    attend_tiles(0, OVER)
    finish(att, acc)
    loads[8].wait()
    loads[9].wait()
    for b in range(2):
        project(0, b, att, sowv, 2, True)
    crossed(0, 2, 3)
    attend_guide(0, 1)
    hop(1, 1, 2)
    crossed(0, 4, 5, 6, 7)
    attend_guide(0, 2, 3)
    finish(gud, acc2)
    for b in range(2):
        project(0, b, gud, cowv, 3, False)
        send(psend.at[0, rows(b)], precv.at[rows(b)], ps.at[0, b], pr.at[0, b], "head")
    hop(1, 3, 4)

    loads[10].wait()
    remote(known, knownv.at[1 - h], kss.at[0], krs.at[0], "head").wait_recv()
    for b in range(2):
        r = rows(b)
        remote(psend.at[0, r], precv.at[r], ps.at[0, b], pr.at[0, b], "head").wait_recv()
        for n in range(2):
            cols = slice(HALF * n, HALF * (n + 1))
            noise = part[r, cols] + precv[r, cols].astype(F32)
            statev[n, r] = updated(0, b, n, latv[n, r].astype(F32), noise)
        mix(1, b, statev)
        keys_values(1, b)
        if b == 0:
            hop(1, 5, 6)
    hop(1, 7)
    queries(plainb, cwv, cqs, False)
    queries(mixb, swv, qs, True)
    crossed(1, *range(8))
    attend_guide(1, 0, 1)
    relay(1, 0)
    attend_guide(1, 2, 3)
    finish(gud, acc2)
    for b in range(2):
        project(1, b, gud, cowv, 3, True)
    relay(1, 1)
    mine = pl.ds(pl.multiple_of(HALF * h, HALF), HALF)
    theirs = pl.ds(pl.multiple_of(HALF * (1 - h), HALF), HALF)
    for slot in (CORE, OVER):
        for b in range(2):
            arrived(1, slot, b)
    for b in range(2):
        attend_listed(1, b)
        project(1, b, att, sowv, 2, False)
        send(psend.at[1, rows(b), theirs], pfin.at[rows(b)], ps.at[1, b], pr.at[1, b], "head")
    for b in range(2):
        r = rows(b)
        remote(psend.at[1, r, theirs], pfin.at[r], ps.at[1, b], pr.at[1, b], "head").wait_recv()
        noise = part[r, mine] + pfin[r].astype(F32)
        out[r] = updated(1, b, h, statev[h, r].astype(F32), noise)

    for copy in sent:
        copy.wait_send()


def on_device(
    latents, known, seam_mask, timesteps, block_lists, guidance,
    modulation_weight, self_weight, self_out_weight, cross_weight, cross_out_weight,
):
    vmem = pl.BlockSpec(memory_space=pltpu.VMEM)
    smem = pl.BlockSpec(memory_space=pltpu.SMEM)
    hbm = pl.BlockSpec(memory_space=pl.ANY)
    dma = lambda *shape: pltpu.SemaphoreType.DMA(shape)
    return pl.pallas_call(
        kernel,
        out_shape=jax.ShapeDtypeStruct((TOK, HALF), BF16),
        in_specs=[smem, smem, vmem, vmem] + [hbm] * 7,
        out_specs=vmem,
        scratch_shapes=[
            pltpu.VMEM((2, TOK, HALF), BF16),
            pltpu.VMEM((2, TOK, HALF), BF16),
            pltpu.VMEM((2, TOK, HALF), BF16),
            pltpu.VMEM((FREQ, 4, D), BF16),
            pltpu.VMEM((3, D, HALF), BF16),
            pltpu.VMEM((HALF, D), BF16),
            pltpu.VMEM((3, D, HALF), BF16),
            pltpu.VMEM((HALF, D), BF16),
            pltpu.VMEM((STEPS, FREQ, BLOCK), F32),
            pltpu.VMEM((2, 16, BLOCK), F32),
            pltpu.VMEM((2, 16, BLOCK), F32),
            pltpu.VMEM((TOK, BLOCK), F32),
            pltpu.VMEM((STEPS, 4, D), F32),
            pltpu.VMEM((TOK, D), BF16),
            pltpu.VMEM((TOK, D), BF16),
            pltpu.VMEM((10, BLOCK, D), BF16),
            pltpu.VMEM((10, BLOCK, D), BF16),
            pltpu.VMEM((2, STEPS, 8, BLOCK, HALF), BF16),
            pltpu.VMEM((STEPS, BLOCK, HALF), BF16),
            pltpu.VMEM((4, STEPS * GUIDE, D), BF16),
            pltpu.VMEM((8, TOK, BLOCK), BF16),
            pltpu.VMEM((8, TOK, BLOCK), BF16),
            pltpu.VMEM((8, HEAD_DIM + 16, TOK), F32),
            pltpu.VMEM((8, 8, TOK), F32),
            pltpu.VMEM((8, HEAD_DIM + 16, TOK), F32),
            pltpu.VMEM((8, 8, TOK), F32),
            pltpu.VMEM((TOK, HALF), BF16),
            pltpu.VMEM((TOK, HALF), BF16),
            pltpu.VMEM((TOK, D), F32),
            pltpu.VMEM((STEPS, TOK, D), BF16),
            pltpu.VMEM((TOK, D), BF16),
            pltpu.VMEM((TOK, HALF), BF16),
            dma(11), dma(2), dma(2), dma(1), dma(1),
            dma(STEPS, 4, 2, 2), dma(STEPS, 5, 2, 2),
            dma(3), dma(3), dma(STEPS, 3), dma(STEPS, 3),
            dma(STEPS, 8), dma(STEPS, 8), dma(STEPS, 8), dma(STEPS, 8),
            dma(STEPS, 2), dma(STEPS, 2),
        ],
        compiler_params=pltpu.CompilerParams(
            collective_id=0, has_side_effects=True, vmem_limit_bytes=56 << 20
        ),
        name="denoise",
    )(
        timesteps, block_lists, seam_mask, guidance.reshape(STEPS * GUIDE, D),
        latents, known, modulation_weight, jnp.transpose(self_weight, (1, 0, 2)),
        self_out_weight, jnp.transpose(cross_weight, (1, 0, 2)), cross_out_weight,
    )


def solution(mesh):
    in_specs = (
        P("seq", "head"), P("seq", "head"), P("seq"), P(), P("seq", None), P(None, "seq", None),
        P(), P(None, None, "head"), P("head", None), P(None, None, "head"), P("head", None),
    )
    return jax.shard_map(
        on_device, mesh=mesh, in_specs=in_specs, out_specs=P("seq", "head"), check_vma=False
    )
```
